256 devices in a mesh: row: 32 (over x_lo, z, core), blk: 8 (over y, x_hi).
Axes of the slice: x: 4 (x_hi: 2, x_lo: 2; x = x_hi * 2 + x_lo), y: 4, z: 8, core: 2. Of those that a mesh axis runs over, the one named last changes fastest.
Arguments:
- embeddings: bfloat16 [65536, 192], P(('row', 'blk')), may hold values from -30 to 30
- vectors: float32 [65536, 16], P(('row', 'blk')), may hold values from -6 to 6
Outputs:
- basis: float32 [65536, 16], P(('row', 'blk'))
- triangle: float32 [16, 16], replicated
The draws below stay inside these ranges and needn't reach their ends.
All inputs are finite; a program needn't handle non-finite values.
Results may differ from the reference program's by a relative error of at most 0.0088.
Values may be sent and summed in bfloat16 or wider, within the bound.
No kernel may reach another device: no remote copies, remote signals or barrier semaphores. Data moves between devices by JAX's collectives and lax.ppermute only.
A program may use at most 64 MiB of HBM per device.

```python
import math
import jax
import jax.numpy as jnp
from jax import lax

DIM = 192
VEC = 16
SEGMENTS = 65536


voices = 48


rooms = 4


def draw_embeddings(key, part):
    keys = jax.random.split(jax.random.fold_in(key, 11), 7)
    labels = jax.random.randint(keys[0], (SEGMENTS,), 0, voices)
    places = jax.random.randint(keys[1], (SEGMENTS,), 0, rooms)
    centres = jax.random.normal(keys[2], (voices, DIM), jnp.float32)
    room_dirs = jax.random.normal(keys[3], (rooms, DIM), jnp.float32)
    strength = jax.random.uniform(keys[4], (SEGMENTS, 1), jnp.float32, 0.2, 1.5)
    channel = jax.random.uniform(keys[5], (SEGMENTS, 1), jnp.float32, 0.0, 1.0)
    noise = jax.random.normal(keys[6], (SEGMENTS, DIM), jnp.float32)
    values = 1.5 * strength * centres[labels] + channel * room_dirs[places] + noise
    return jnp.clip(values, -30.0, 30.0).astype(jnp.bfloat16)


def draw_vectors(key, part):
    first, second, third = jax.random.split(jax.random.fold_in(key, 23), 3)
    signs = jnp.where(jax.random.bernoulli(second, 0.5, (VEC,)), 1.0, -1.0)
    offsets = jax.random.uniform(first, (VEC,), jnp.float32, 0.5, 1.0) * signs
    noise = jnp.clip(jax.random.normal(third, (SEGMENTS, VEC), jnp.float32), -4.0, 4.0)
    return jnp.clip(noise + offsets[None, :], -6.0, 6.0)


def setup_inputs(seed: int = 0) -> dict:
    arg_keys = jax.random.split(jax.random.key(seed), 3)
    return {
        "embeddings": draw_embeddings(jax.random.fold_in(arg_keys[2], 71), 0),
        "vectors": draw_vectors(jax.random.fold_in(arg_keys[2], 71), 0),
    }


sharpness = 10.0
epsilon = 1e-06

def normalize(embeddings):
    values = embeddings.astype(jnp.float32)
    return (values * lax.rsqrt(lax.optimization_barrier(jnp.sum(values * values, axis=1, keepdims=True)) + epsilon)).astype(jnp.bfloat16)

def affinity(block_rows, columns):
    scores = lax.dot_general(block_rows.astype(jnp.float32), columns.astype(jnp.float32), (((1,), (1,)), ((), ())), preferred_element_type=jnp.float32)
    return jnp.exp(sharpness * (scores - 1.0))

def reference(embeddings, vectors):
    unit_rows = normalize(embeddings)
    total = unit_rows.shape[0]
    blocks = unit_rows.reshape(-1, math.gcd(total, 512), unit_rows.shape[1])

    def degree_block(block_rows):
        return lax.optimization_barrier(jnp.sum(affinity(block_rows, unit_rows), axis=1))
    degree = lax.map(degree_block, blocks).reshape(total)
    inverse_root = lax.rsqrt(degree)
    weighted = (vectors * inverse_root[:, None]).astype(jnp.bfloat16)

    def apply_block(block_rows):
        tile = affinity(block_rows, unit_rows).astype(jnp.bfloat16)
        return jnp.dot(tile.astype(jnp.float32), weighted.astype(jnp.float32), preferred_element_type=jnp.float32)
    summed = lax.map(apply_block, blocks).reshape(total, vectors.shape[1])
    projected = summed * inverse_root[:, None]
    gram_matrix = jnp.dot(projected.T, projected, precision=lax.Precision.HIGHEST)
    factor = jnp.linalg.cholesky(gram_matrix)
    basis = jax.scipy.linalg.solve_triangular(factor, projected.T, lower=True).T
    return (basis, factor.T)
```

```python
import functools

import jax
import jax.numpy as jnp
from jax import lax
from jax.experimental import pallas as pl
from jax.experimental.pallas import tpu as pltpu
from jax.sharding import Mesh
from jax.sharding import PartitionSpec as P

AXES = ("xl", "z", "core", "y", "xh")
SIZES = (2, 8, 2, 4, 2)
ROWS = ("z", "core")
COLS = ("xl", "y", "xh")
NR = 16
NC = 16
SEG = 256
DIM = 192
VEC = 16
WIDE = DIM + 2 * VEC
SCALE = 14.426950408889634
EPS = 1e-6
MIB = 1 << 20
F32 = jnp.float32
BF16 = jnp.bfloat16
HI = lax.Precision.HIGHEST


def params(mib):
    return pltpu.CompilerParams(vmem_limit_bytes=mib * MIB)


def vmem():
    return pl.BlockSpec(memory_space=pltpu.VMEM)


def smem():
    return pl.BlockSpec(memory_space=pltpu.SMEM)


def nt(a, b, **kw):
    return lax.dot_general(a, b, (((1,), (1,)), ((), ())), preferred_element_type=F32, **kw)


def unit_kernel(e_ref, v_ref, o_ref, many_ref):
    e = e_ref[...].astype(F32)
    u = e * lax.rsqrt(jnp.sum(e * e, axis=1, keepdims=True) + EPS)
    o_ref[0:DIM, :] = u.T.astype(BF16)
    v = v_ref[...].T
    hi = v.astype(BF16)
    o_ref[DIM : DIM + VEC, :] = hi
    o_ref[DIM + VEC : WIDE, :] = (v - hi.astype(F32)).astype(BF16)
    for k in range(NC):
        many_ref[k] = o_ref[...]


def affinity_kernel(pos_ref, t_ref, *refs):
    near, far = refs[0:8], refs[8:16]
    b_ref, deg_ref, s_ref = refs[16:19]
    z, core = pos_ref[0], pos_ref[1]
    for k in range(8):
        zz = lax.rem(z + 8 - k, 8)
        s_ref[zz * 2 + core] = near[k][0:DIM, :]
        s_ref[zz * 2 + 1 - core] = far[k][0:DIM, :]

    def column_piece(t, carry):
        lhs = t_ref[t, 0:DIM, :].T
        total = jnp.zeros((SEG, 128), F32)
        for s in range(NR):
            score = jnp.dot(lhs, s_ref[s], preferred_element_type=F32)
            tile = jnp.exp2(score * SCALE - SCALE)
            total = total + tile[:, 0:128] + tile[:, 128:256]
            b_ref[s, pl.ds(t * SEG, SEG), :] = tile.astype(BF16)
        sums = nt(jnp.ones((8, 128), F32), total, precision=HI)
        deg_ref[0, pl.ds(t, 1), :] = sums[0:1, :]
        return carry

    lax.fori_loop(0, NC, column_piece, 0)
    for k in range(1, NC):
        deg_ref[k] = deg_ref[0]


def apply_kernel(pos_ref, deg_ref, t_ref, b_ref, p_ref, own_ref, root_ref, w_ref):
    root_ref[...] = lax.rsqrt(jnp.sum(deg_ref[...], axis=0))
    own_ref[...] = root_ref[pl.ds(pos_ref[0], 1), :]
    for t in range(NC):
        v = t_ref[t, DIM : DIM + VEC, :].astype(F32) + t_ref[t, DIM + VEC : WIDE, :].astype(F32)
        w_ref[:, t * SEG : (t + 1) * SEG] = (v * root_ref[t : t + 1, :]).astype(BF16)

    def row_piece(s, carry):
        p_ref[s] = jnp.dot(w_ref[...], b_ref[s], preferred_element_type=F32)
        return carry

    lax.fori_loop(0, NR, row_piece, 0)


def project_kernel(p_ref, own_ref, q_ref, gram_ref):
    q = jnp.sum(p_ref[...], axis=0) * own_ref[...]
    q_ref[...] = q
    gram = nt(q, q, precision=HI)
    for k in range(NR):
        gram_ref[k] = gram


def finish(q, gram):
    factor = jnp.linalg.cholesky(gram)
    basis = jax.scipy.linalg.solve_triangular(factor, q, lower=True).T
    return (basis, factor.T)


def to_all(copies, axes):
    return lax.all_to_all(copies, axes, split_axis=0, concat_axis=0, tiled=True)


def shape(*dims, dtype=F32):
    return jax.ShapeDtypeStruct(dims, dtype)


def per_device(embeddings, vectors):
    z, core = lax.axis_index("z"), lax.axis_index("core")
    column = lax.axis_index(COLS)
    unit, unit_copies = pl.pallas_call(
        unit_kernel,
        out_shape=(shape(WIDE, SEG, dtype=BF16), shape(NC, WIDE, SEG, dtype=BF16)),
        name="unit",
    )(embeddings, vectors)
    near = [unit]
    for k in range(1, 8):
        near.append(lax.ppermute(unit, "z", [(i, (i + k) % 8) for i in range(8)]))
    far = [lax.ppermute(a, "core", [(0, 1), (1, 0)]) for a in near]
    columns = to_all(unit_copies, COLS)
    block, degree = pl.pallas_call(
        affinity_kernel,
        out_shape=(shape(NR, NC * SEG, SEG, dtype=BF16), shape(NC, NC, SEG)),
        in_specs=[smem()] + [vmem()] * 17,
        out_specs=(vmem(), vmem()),
        scratch_shapes=[pltpu.VMEM((NR, DIM, SEG), BF16)],
        compiler_params=params(56),
        name="affinity",
    )(jnp.stack([z, core]), columns, *near, *far)
    degree = to_all(degree, COLS)
    product, own = pl.pallas_call(
        apply_kernel,
        out_shape=(shape(NR, VEC, SEG), shape(1, SEG)),
        in_specs=[smem(), vmem(), vmem(), vmem()],
        out_specs=(vmem(), vmem()),
        scratch_shapes=[pltpu.VMEM((NC, SEG), F32), pltpu.VMEM((VEC, NC * SEG), BF16)],
        compiler_params=params(56),
        name="apply",
    )(jnp.stack([column]), degree, columns, block)
    product = to_all(product, ROWS)
    projected, gram = pl.pallas_call(
        project_kernel,
        out_shape=(shape(VEC, SEG), shape(NR, VEC, VEC)),
        name="project",
    )(product, own)
    gram = jnp.sum(to_all(gram, ROWS), axis=0)
    gram = jnp.sum(to_all(jnp.broadcast_to(gram, (NC, VEC, VEC)), COLS), axis=0)
    return finish(projected, gram)


def solution(mesh):
    torus = Mesh(mesh.devices.reshape(SIZES), AXES)
    placed = (P(AXES, None), P(AXES, None))
    return jax.shard_map(
        per_device, mesh=torus, in_specs=placed, out_specs=(P(AXES, None), P()), check_vma=False
    )
```

```python
import jax
import jax.numpy as jnp
from jax import lax
from jax.experimental import pallas as pl
from jax.experimental.pallas import tpu as pltpu
from jax.sharding import Mesh
from jax.sharding import PartitionSpec as P

AXES = ("xl", "z", "core", "y", "xh")
SIZES = (2, 8, 2, 4, 2)
ROWS = ("z", "core")
COLS = ("xl", "y", "xh")
ALL = 256
NR = 16
NC = 16
SEG = 256
DIM = 192
VEC = 16
SCALE = 14.426950408889634
EPS = 1e-6
MIB = 1 << 20
F32 = jnp.float32
BF16 = jnp.bfloat16
HI = lax.Precision.HIGHEST


def params(mib):
    return pltpu.CompilerParams(vmem_limit_bytes=mib * MIB)


def vmem():
    return pl.BlockSpec(memory_space=pltpu.VMEM)


def smem():
    return pl.BlockSpec(memory_space=pltpu.SMEM)


def nt(a, b, **kw):
    return lax.dot_general(a, b, (((1,), (1,)), ((), ())), preferred_element_type=F32, **kw)


def unit_kernel(e_ref, u_ref, many_ref):
    e = e_ref[...].astype(F32)
    u_ref[...] = (e * lax.rsqrt(jnp.sum(e * e, axis=0, keepdims=True) + EPS)).astype(BF16)
    for k in range(NC):
        many_ref[k] = u_ref[...]


def affinity_kernel(pos_ref, t_ref, *refs):
    near, far = refs[0:8], refs[8:16]
    b_ref, deg_ref, s_ref, c_ref, acc_ref = refs[16:21]
    z, core = pos_ref[0], pos_ref[1]
    step = pl.program_id(0)

    @pl.when(step == 0)
    def _():
        for k in range(8):
            zz = lax.rem(z + 8 - k, 8)
            s_ref[zz * 2 + core] = near[k][...]
            s_ref[zz * 2 + 1 - core] = far[k][...]
        for t in range(NC):
            c_ref[t] = t_ref[t].T
        acc_ref[...] = jnp.zeros_like(acc_ref)

    for t in range(NC):
        total = acc_ref[t]
        for j in range(2):
            score = jnp.dot(c_ref[t], s_ref[step * 2 + j], preferred_element_type=F32)
            tile = jnp.exp2(score * SCALE)
            total = total + (tile[:, 0:128] + tile[:, 128:256])
            b_ref[j, t * SEG : (t + 1) * SEG, :] = tile.astype(BF16)
        acc_ref[t] = total

    @pl.when(step == NR // 2 - 1)
    def _():
        for t in range(NC):
            sums = nt(jnp.ones((8, 128), F32), acc_ref[t], precision=HI)
            deg_ref[0, t : t + 1, :] = sums[0:1, :]
        for k in range(1, NC):
            deg_ref[k] = deg_ref[0]


def apply_kernel(pos_ref, deg_ref, v_ref, b_ref, p_ref, own_ref, root_ref, w_ref):
    @pl.when(pl.program_id(0) == 0)
    def _():
        root_ref[...] = lax.rsqrt(jnp.sum(deg_ref[...], axis=0))
        own_ref[...] = root_ref[pl.ds(pos_ref[0], 1), :]
        for t in range(NC):
            w_ref[:, t * SEG : (t + 1) * SEG] = (v_ref[t] * root_ref[t : t + 1, :]).astype(BF16)

    p_ref[0] = jnp.dot(w_ref[...], b_ref[0], preferred_element_type=F32)


def project_kernel(p_ref, own_ref, q_ref, gram_ref):
    q = jnp.sum(p_ref[...], axis=0) * own_ref[...]
    q_ref[...] = q
    down = jnp.concatenate([jnp.broadcast_to(q[a : a + 1], (VEC, SEG)) for a in range(VEC)], axis=0)
    pairs = down * jnp.concatenate([q] * VEC, axis=0)
    gram = nt(jnp.ones((8, SEG), F32), pairs, precision=HI)[0:1]
    flat = jnp.concatenate([gram[:, 0:128], gram[:, 128:256]], axis=0)
    gram_ref[...] = jnp.broadcast_to(flat[None], (ALL, 2, 128))


def finish_kernel(gram_ref, q_ref, basis_ref, triangle_ref):
    flat = jnp.sum(gram_ref[...], axis=0)
    row = lax.broadcasted_iota(jnp.int32, (VEC, 128), 0)
    lane = lax.broadcasted_iota(jnp.int32, (VEC, 128), 1)
    low = jnp.where(lane // VEC == row, flat[0:1], 0.0)
    high = jnp.where(lane // VEC == row - 8, flat[1:2], 0.0)
    pick = jnp.where(
        lax.broadcasted_iota(jnp.int32, (128, 128), 0) % VEC
        == lax.broadcasted_iota(jnp.int32, (128, 128), 1),
        1.0,
        0.0,
    )
    g = jnp.dot(low + high, pick, preferred_element_type=F32, precision=HI)
    q = q_ref[...]
    wide = lax.broadcasted_iota(jnp.int32, (VEC, SEG), 0)
    for k in range(VEC):
        column = jnp.sum(jnp.where(lane == k, g, 0.0), axis=1, keepdims=True)
        inverse = lax.rsqrt(column[k : k + 1, :])
        factor = column * inverse
        top_g = g[k : k + 1, :] * inverse
        top_q = q[k : k + 1, :] * inverse
        g = jnp.where(row == k, top_g, jnp.where(row > k, g - factor * top_g, g))
        q = jnp.where(wide == k, top_q, jnp.where(wide > k, q - factor * top_q, q))
    basis_ref[...] = q
    triangle_ref[...] = jnp.where(lane >= row, g, 0.0)[:, 0:VEC]


def to_all(copies, axes):
    return lax.all_to_all(copies, axes, split_axis=0, concat_axis=0, tiled=True)


def shape(*dims, dtype=F32):
    return jax.ShapeDtypeStruct(dims, dtype)


def per_device(embeddings, vectors):
    z, core = lax.axis_index("z"), lax.axis_index("core")
    column = lax.axis_index(COLS)
    unit, unit_copies = pl.pallas_call(
        unit_kernel,
        out_shape=(shape(DIM, SEG, dtype=BF16), shape(NC, DIM, SEG, dtype=BF16)),
        name="unit",
    )(embeddings.T)
    near = [unit]
    for k in range(1, 8):
        near.append(lax.ppermute(unit, "z", [(i, (i + k) % 8) for i in range(8)]))
    far = [lax.ppermute(a, "core", [(0, 1), (1, 0)]) for a in near]
    columns = to_all(unit_copies, COLS)
    vector_columns = to_all(jnp.broadcast_to(vectors.T, (NC, VEC, SEG)), COLS)
    block, degree = pl.pallas_call(
        affinity_kernel,
        grid=(NR // 2,),
        out_shape=(shape(NR, NC * SEG, SEG, dtype=BF16), shape(NC, NC, SEG)),
        in_specs=[smem()] + [vmem()] * 17,
        out_specs=(pl.BlockSpec((2, NC * SEG, SEG), lambda i: (i, 0, 0)), vmem()),
        scratch_shapes=[
            pltpu.VMEM((NR, DIM, SEG), BF16),
            pltpu.VMEM((NC, SEG, DIM), BF16),
            pltpu.VMEM((NC, SEG, 128), F32),
        ],
        compiler_params=params(32),
        cost_estimate=pl.CostEstimate(
            flops=2 * 256 * 4096 * 4096, transcendentals=4096 * 4096, bytes_accessed=1 << 23
        ),
        name="affinity",
    )(jnp.stack([z, core]), columns, *near, *far)
    degree = to_all(degree, COLS)
    product, own = pl.pallas_call(
        apply_kernel,
        out_shape=(shape(NR, VEC, SEG), shape(1, SEG)),
        grid=(NR,),
        in_specs=[smem(), vmem(), vmem(), pl.BlockSpec((1, NC * SEG, SEG), lambda i: (i, 0, 0))],
        out_specs=(pl.BlockSpec((1, VEC, SEG), lambda i: (i, 0, 0)), vmem()),
        scratch_shapes=[pltpu.VMEM((NC, SEG), F32), pltpu.VMEM((VEC, NC * SEG), BF16)],
        compiler_params=params(44),
        name="apply",
    )(jnp.stack([column]), degree, vector_columns, block)
    product = to_all(product, ROWS)
    projected, gram = pl.pallas_call(
        project_kernel,
        out_shape=(shape(VEC, SEG), shape(ALL, 2, 128)),
        name="project",
    )(product, own)
    gram = to_all(gram, AXES)
    basis, triangle = pl.pallas_call(
        finish_kernel,
        out_shape=(shape(VEC, SEG), shape(VEC, VEC)),
        name="finish",
    )(gram, projected)
    return basis.T, triangle


def solution(mesh):
    torus = Mesh(mesh.devices.reshape(SIZES), AXES)
    placed = (P(AXES, None), P(AXES, None))
    return jax.shard_map(
        per_device, mesh=torus, in_specs=placed, out_specs=(P(AXES, None), P()), check_vma=False
    )
```

```python
import jax
import jax.numpy as jnp
from jax import lax
from jax.experimental import pallas as pl
from jax.experimental.pallas import tpu as pltpu
from jax.sharding import Mesh
from jax.sharding import PartitionSpec as P

AXES = ("xl", "z", "core", "y", "xh")
SIZES = (2, 8, 2, 4, 2)
ROWS = ("z", "core")
COLS = ("xl", "y", "xh")
CHIPS = 128
NR = 16
NC = 16
SEG = 256
DIM = 192
VEC = 16
WIDE = DIM + 2 * VEC
DEPTH = 6
SCALE = 14.426950408889634
UNSCALE = 4.5399929762484854e-05
EPS = 1e-6
MIB = 1 << 20
F32 = jnp.float32
BF16 = jnp.bfloat16
HI = lax.Precision.HIGHEST


def params(mib):
    return pltpu.CompilerParams(vmem_limit_bytes=mib * MIB)


def vmem():
    return pl.BlockSpec(memory_space=pltpu.VMEM)


def smem():
    return pl.BlockSpec(memory_space=pltpu.SMEM)


def nt(a, b, **kw):
    return lax.dot_general(a, b, (((1,), (1,)), ((), ())), preferred_element_type=F32, **kw)


def unit_kernel(e_ref, v_ref, u_ref, many_ref):
    e = e_ref[...].astype(F32)
    u = (e * lax.rsqrt(jnp.sum(e * e, axis=0, keepdims=True) + EPS)).astype(BF16)
    u_ref[...] = u
    v = v_ref[...]
    high = v.astype(BF16)
    low = (v - high.astype(F32)).astype(BF16)
    for k in range(NC):
        many_ref[k, 0:DIM, :] = u
        many_ref[k, DIM : DIM + VEC, :] = high
        many_ref[k, DIM + VEC : WIDE, :] = low


def affinity_kernel(pos_ref, t_ref, *refs):
    pairs, lone = refs[0:7], refs[7:9]
    b_ref, deg_ref, s_ref = refs[9:12]
    z, core = pos_ref[0], pos_ref[1]
    step = pl.program_id(0)

    def place(chip, side, rows):
        s_ref[lax.rem(chip + 16, 8) * 2 + side] = rows.T

    @pl.when(step == 0)
    def _():
        sign = 1 - 2 * core
        place(z, core, pairs[0][0])
        place(z, 1 - core, pairs[0][1])
        for k in range(1, 4):
            place(z - k * sign, core, pairs[2 * k - 1][0])
            place(z - k * sign, 1 - core, pairs[2 * k - 1][1])
            place(z + k * sign, 1 - core, pairs[2 * k][0])
            place(z + k * sign, core, pairs[2 * k][1])
        place(z + 4, core, lone[0][...])
        place(z + 4, 1 - core, lone[1][...])

    for j in range(2):
        piece = t_ref[step * 2 + j, 0:DIM, :]
        total = jnp.zeros((8, SEG), F32)
        for r in range(NR):
            score = jnp.dot(s_ref[r], piece, preferred_element_type=F32)
            tile = jnp.exp2(score * SCALE)
            total = total + jnp.sum(tile.reshape(SEG // 8, 8, SEG), axis=0)
            b_ref[j, r * SEG : (r + 1) * SEG, :] = tile.astype(BF16)
        sums = jnp.sum(total, axis=0, keepdims=True) * UNSCALE
        for k in range(NC):
            deg_ref[k, pl.ds(step * 2 + j, 1), :] = sums


def apply_kernel(pos_ref, deg_ref, t_ref, b_ref, p_ref, own_ref, root_ref, held_ref, sem_ref):
    def fetch(t):
        slot = t % DEPTH
        return pltpu.make_async_copy(b_ref.at[t], held_ref.at[slot], sem_ref.at[slot])

    for t in range(DEPTH):
        fetch(t).start()
    root_ref[...] = lax.rsqrt(jnp.sum(deg_ref[...], axis=0))
    own_ref[...] = root_ref[pl.ds(pos_ref[0], 1), :] * UNSCALE
    for t in range(NC):
        v = t_ref[t, DIM : DIM + VEC, :].astype(F32) + t_ref[t, DIM + VEC : WIDE, :].astype(F32)
        w = (v * root_ref[t : t + 1, :]).astype(BF16)
        fetch(t).wait()
        for r in range(NR):
            part = nt(w, held_ref[t % DEPTH, r * SEG : (r + 1) * SEG, :])
            p_ref[r] = part if t == 0 else p_ref[r] + part
        if t + DEPTH < NC:
            fetch(t + DEPTH).start()


def project_kernel(p_ref, own_ref, q_ref, gram_ref):
    q = jnp.sum(p_ref[...], axis=0) * own_ref[...]
    q_ref[...] = q
    down = jnp.concatenate([jnp.broadcast_to(q[a : a + 1], (VEC, SEG)) for a in range(VEC)], axis=0)
    pairs = down * jnp.concatenate([q] * VEC, axis=0)
    gram = nt(jnp.ones((8, SEG), F32), pairs, precision=HI)[0:1]
    flat = jnp.concatenate([gram[:, 0:128], gram[:, 128:256]], axis=0)
    gram_ref[...] = flat


def finish_kernel(gram_ref, q_ref, basis_ref, triangle_ref):
    flat = jnp.sum(gram_ref[...], axis=0)
    row = lax.broadcasted_iota(jnp.int32, (VEC, 128), 0)
    lane = lax.broadcasted_iota(jnp.int32, (VEC, 128), 1)
    low = jnp.where(lane // VEC == row, flat[0:1], 0.0)
    high = jnp.where(lane // VEC == row - 8, flat[1:2], 0.0)
    pick = jnp.where(
        lax.broadcasted_iota(jnp.int32, (128, 128), 0) % VEC
        == lax.broadcasted_iota(jnp.int32, (128, 128), 1),
        1.0,
        0.0,
    )
    g = jnp.dot(low + high, pick, preferred_element_type=F32, precision=HI)
    q = q_ref[...]
    wide = lax.broadcasted_iota(jnp.int32, (VEC, SEG), 0)
    for k in range(VEC):
        column = jnp.sum(jnp.where(lane == k, g, 0.0), axis=1, keepdims=True)
        inverse = lax.rsqrt(column[k : k + 1, :])
        factor = column * inverse
        top_g = g[k : k + 1, :] * inverse
        top_q = q[k : k + 1, :] * inverse
        g = jnp.where(row == k, top_g, jnp.where(row > k, g - factor * top_g, g))
        q = jnp.where(wide == k, top_q, jnp.where(wide > k, q - factor * top_q, q))
    basis_ref[...] = q
    triangle_ref[...] = jnp.where(lane >= row, g, 0.0)[:, 0:VEC]


def to_all(copies, axes):
    return lax.all_to_all(copies, axes, split_axis=0, concat_axis=0, tiled=True)


def shape(*dims, dtype=F32):
    return jax.ShapeDtypeStruct(dims, dtype)


def across(a):
    return lax.ppermute(a, "core", [(0, 1), (1, 0)])


def along(a, hops):
    turns = []
    for z in range(8):
        turns += [(z * 2, (z + hops) % 8 * 2), (z * 2 + 1, (z - hops) % 8 * 2 + 1)]
    return lax.ppermute(a, ROWS, turns)


def per_device(embeddings, vectors):
    z, core = lax.axis_index("z"), lax.axis_index("core")
    column = lax.axis_index(COLS)
    unit, unit_copies = pl.pallas_call(
        unit_kernel,
        out_shape=(shape(DIM, SEG, dtype=BF16), shape(NC, WIDE, SEG, dtype=BF16)),
        name="unit",
    )(embeddings.T, vectors.T)
    columns = to_all(unit_copies, COLS)
    pair = jnp.stack([unit, across(unit)])
    one, two = along(pair, 1), along(pair, 2)
    three, four = along(two, 1), along(two[0], 2)
    pairs = (pair, one, across(one), two, across(two), three, across(three))
    block, degree = pl.pallas_call(
        affinity_kernel,
        grid=(NC // 2,),
        out_shape=(shape(NC, NR * SEG, SEG, dtype=BF16), shape(NC, NC, SEG)),
        in_specs=[smem()] + [vmem()] * 10,
        out_specs=(pl.BlockSpec((2, NR * SEG, SEG), lambda i: (i, 0, 0)), vmem()),
        scratch_shapes=[pltpu.VMEM((NR, SEG, DIM), BF16)],
        compiler_params=params(32),
        cost_estimate=pl.CostEstimate(
            flops=2 * 256 * 4096 * 4096, transcendentals=4096 * 4096, bytes_accessed=1 << 25
        ),
        name="affinity",
    )(jnp.stack([z, core]), columns, *pairs, four, across(four))
    degree = to_all(degree, COLS)
    product, own = pl.pallas_call(
        apply_kernel,
        out_shape=(shape(NR, VEC, SEG), shape(1, SEG)),
        in_specs=[smem(), vmem(), vmem(), pl.BlockSpec(memory_space=pl.ANY)],
        out_specs=(vmem(), vmem()),
        scratch_shapes=[
            pltpu.VMEM((NC, SEG), F32),
            pltpu.VMEM((DEPTH, NR * SEG, SEG), BF16),
            pltpu.SemaphoreType.DMA((DEPTH,)),
        ],
        compiler_params=params(44),
        name="apply",
    )(jnp.stack([column]), degree, columns, block)
    product = to_all(product, ROWS)
    projected, gram = pl.pallas_call(
        project_kernel,
        out_shape=(shape(VEC, SEG), shape(2, 128)),
        name="project",
    )(product, own)
    gram = jnp.broadcast_to(gram + across(gram), (CHIPS, 2, 128))
    gram = to_all(gram, ("xl", "z", "y", "xh"))
    basis, triangle = pl.pallas_call(
        finish_kernel,
        out_shape=(shape(VEC, SEG), shape(VEC, VEC)),
        name="finish",
    )(gram, projected)
    return basis.T, triangle


def solution(mesh):
    torus = Mesh(mesh.devices.reshape(SIZES), AXES)
    placed = (P(AXES, None), P(AXES, None))
    return jax.shard_map(
        per_device, mesh=torus, in_specs=placed, out_specs=(P(AXES, None), P()), check_vma=False
    )
```

```python
import jax
import jax.numpy as jnp
from jax import lax
from jax.experimental import pallas as pl
from jax.experimental.pallas import tpu as pltpu
from jax.sharding import Mesh
from jax.sharding import PartitionSpec as P

AXES = ("xl", "z", "core", "y", "xh")
SIZES = (2, 8, 2, 4, 2)
ROWS = ("z", "core")
COLS = ("xl", "y", "xh")
CHIPS = 128
HALF = 8
NR = 16
NC = 16
SEG = 256
DIM = 192
VEC = 16
WIDE = DIM + 2 * VEC
DEPTH = 6
SCALE = 14.426950408889634
UNSCALE = 4.5399929762484854e-05
EPS = 1e-6
MIB = 1 << 20
F32 = jnp.float32
BF16 = jnp.bfloat16
HI = lax.Precision.HIGHEST


def params(mib):
    return pltpu.CompilerParams(vmem_limit_bytes=mib * MIB)


def vmem():
    return pl.BlockSpec(memory_space=pltpu.VMEM)


def smem():
    return pl.BlockSpec(memory_space=pltpu.SMEM)


def nt(a, b, **kw):
    return lax.dot_general(a, b, (((1,), (1,)), ((), ())), preferred_element_type=F32, **kw)


def unit_kernel(e_ref, v_ref, u_ref, own_ref, many_ref):
    e = e_ref[...].astype(F32)
    u = (e * lax.rsqrt(jnp.sum(e * e, axis=0, keepdims=True) + EPS)).astype(BF16)
    u_ref[...] = u
    v = v_ref[...]
    high = v.astype(BF16)
    low = (v - high.astype(F32)).astype(BF16)
    own_ref[0:DIM, :] = u
    own_ref[DIM : DIM + VEC, :] = high
    own_ref[DIM + VEC : WIDE, :] = low
    for k in range(HALF):
        many_ref[k] = own_ref[...]


def score_pieces(step, t_ref, s_ref, b_ref, keep):
    for j in range(2):
        t = step * 2 + j
        piece = t_ref[t, 0:DIM, :]
        total = jnp.zeros((8, SEG), F32)
        for r in range(NR):
            score = jnp.dot(s_ref[r], piece, preferred_element_type=F32)
            tile = jnp.exp2(score * SCALE)
            total = total + jnp.sum(tile.reshape(SEG // 8, 8, SEG), axis=0)
            b_ref[j, r * SEG : (r + 1) * SEG, :] = tile.astype(BF16)
        keep(t, jnp.sum(total, axis=0, keepdims=True) * UNSCALE)


def first_kernel(pos_ref, t_ref, *refs):
    pairs, lone = refs[0:7], refs[7:9]
    b_ref, deg_ref, s_ref = refs[9:12]
    z, core = pos_ref[0], pos_ref[1]
    step = pl.program_id(0)

    def place(chip, side, rows):
        s_ref[lax.rem(chip + 16, 8) * 2 + side] = rows.T

    @pl.when(step == 0)
    def _():
        sign = 1 - 2 * core
        place(z, core, pairs[0][0])
        place(z, 1 - core, pairs[0][1])
        for k in range(1, 4):
            place(z - k * sign, core, pairs[2 * k - 1][0])
            place(z - k * sign, 1 - core, pairs[2 * k - 1][1])
            place(z + k * sign, 1 - core, pairs[2 * k][0])
            place(z + k * sign, core, pairs[2 * k][1])
        place(z + 4, core, lone[0][...])
        place(z + 4, 1 - core, lone[1][...])

    def keep(t, sums):
        deg_ref[pl.ds(t, 1), :] = sums

    score_pieces(step, t_ref, s_ref, b_ref, keep)


def second_kernel(pos_ref, t_ref, s_ref, first_ref, b_ref, deg_ref):
    xh = pos_ref[2]
    step = pl.program_id(0)

    @pl.when(step == 0)
    def _():
        for t in range(HALF):
            for k in range(NC):
                deg_ref[k, pl.ds(t * 2 + xh, 1), :] = first_ref[t : t + 1, :]

    def keep(t, sums):
        for k in range(NC):
            deg_ref[k, pl.ds(t * 2 + 1 - xh, 1), :] = sums

    score_pieces(step, t_ref, s_ref, b_ref, keep)


def apply_kernel(pos_ref, deg_ref, *refs):
    columns, blocks = refs[0:2], refs[2:4]
    mine_ref, other_ref, own_ref, root_ref, held_ref, sem_ref = refs[4:10]
    core, xh = pos_ref[1], pos_ref[2]

    def fetch(t):
        slot = t % DEPTH
        return pltpu.make_async_copy(
            blocks[t // HALF].at[t % HALF], held_ref.at[slot], sem_ref.at[slot]
        )

    for t in range(DEPTH):
        fetch(t).start()
    root_ref[...] = lax.rsqrt(jnp.sum(deg_ref[...], axis=0))
    own_ref[...] = root_ref[pl.ds(pos_ref[3], 1), :] * UNSCALE
    for t in range(NC):
        c = t % HALF
        t_ref = columns[t // HALF]
        root = root_ref[pl.ds(c * 2 + (xh if t < HALF else 1 - xh), 1), :]
        v = t_ref[c, DIM : DIM + VEC, :].astype(F32) + t_ref[c, DIM + VEC : WIDE, :].astype(F32)
        w = (v * root).astype(BF16)
        fetch(t).wait()
        for r in range(NR // 2):
            for side, p_ref in ((core, mine_ref), (1 - core, other_ref)):
                rows = pl.ds(pl.multiple_of((r * 2 + side) * SEG, SEG), SEG)
                part = nt(w, held_ref[t % DEPTH, rows, :])
                p_ref[r] = part if t == 0 else p_ref[r] + part
        if t + DEPTH < NC:
            fetch(t + DEPTH).start()


def project_kernel(p_ref, own_ref, q_ref, gram_ref):
    q = jnp.sum(p_ref[...], axis=0) * own_ref[...]
    q_ref[...] = q
    down = jnp.concatenate([jnp.broadcast_to(q[a : a + 1], (VEC, SEG)) for a in range(VEC)], axis=0)
    pairs = down * jnp.concatenate([q] * VEC, axis=0)
    gram = nt(jnp.ones((8, SEG), F32), pairs, precision=HI)[0:1]
    flat = jnp.concatenate([gram[:, 0:128], gram[:, 128:256]], axis=0)
    gram_ref[...] = flat


def finish_kernel(gram_ref, q_ref, basis_ref, triangle_ref):
    flat = jnp.sum(gram_ref[...], axis=0)
    row = lax.broadcasted_iota(jnp.int32, (VEC, 128), 0)
    lane = lax.broadcasted_iota(jnp.int32, (VEC, 128), 1)
    low = jnp.where(lane // VEC == row, flat[0:1], 0.0)
    high = jnp.where(lane // VEC == row - 8, flat[1:2], 0.0)
    pick = jnp.where(
        lax.broadcasted_iota(jnp.int32, (128, 128), 0) % VEC
        == lax.broadcasted_iota(jnp.int32, (128, 128), 1),
        1.0,
        0.0,
    )
    g = jnp.dot(low + high, pick, preferred_element_type=F32, precision=HI)
    q = q_ref[...]
    wide = lax.broadcasted_iota(jnp.int32, (VEC, SEG), 0)
    for k in range(VEC):
        column = jnp.sum(jnp.where(lane == k, g, 0.0), axis=1, keepdims=True)
        inverse = lax.rsqrt(column[k : k + 1, :])
        factor = column * inverse
        top_g = g[k : k + 1, :] * inverse
        top_q = q[k : k + 1, :] * inverse
        g = jnp.where(row == k, top_g, jnp.where(row > k, g - factor * top_g, g))
        q = jnp.where(wide == k, top_q, jnp.where(wide > k, q - factor * top_q, q))
    basis_ref[...] = q
    triangle_ref[...] = jnp.where(lane >= row, g, 0.0)[:, 0:VEC]


def to_all(copies, axes):
    return lax.all_to_all(copies, axes, split_axis=0, concat_axis=0, tiled=True)


def shape(*dims, dtype=F32):
    return jax.ShapeDtypeStruct(dims, dtype)


def across(a):
    return lax.ppermute(a, "core", [(0, 1), (1, 0)])


def along(a, hops):
    turns = []
    for z in range(8):
        turns += [(z * 2, (z + hops) % 8 * 2), (z * 2 + 1, (z - hops) % 8 * 2 + 1)]
    return lax.ppermute(a, ROWS, turns)


def per_device(embeddings, vectors):
    z, core, xh = lax.axis_index("z"), lax.axis_index("core"), lax.axis_index("xh")
    position = jnp.stack([z, core, xh, lax.axis_index(COLS)])
    unit, own_column, copies = pl.pallas_call(
        unit_kernel,
        out_shape=(
            shape(DIM, SEG, dtype=BF16),
            shape(WIDE, SEG, dtype=BF16),
            shape(HALF, WIDE, SEG, dtype=BF16),
        ),
        name="unit",
    )(embeddings.T, vectors.T)
    first_columns = to_all(copies, ("xl", "y"))
    partner = lax.ppermute(own_column, "xh", [(0, 1), (1, 0)])
    second_columns = to_all(jnp.broadcast_to(partner, (HALF, WIDE, SEG)), ("xl", "y"))
    pair = jnp.stack([unit, across(unit)])
    one, two = along(pair, 1), along(pair, 2)
    three, four = along(two, 1), along(two[0], 2)
    pairs = (pair, one, across(one), two, across(two), three, across(three))
    cost = pl.CostEstimate(
        flops=256 * 4096 * 4096, transcendentals=2048 * 4096, bytes_accessed=1 << 24
    )
    half = pltpu.HBM((HALF, NR * SEG, SEG), BF16)
    half_spec = pl.BlockSpec((2, NR * SEG, SEG), lambda i: (i, 0, 0))
    first_block, first_degree, rows = pl.pallas_call(
        first_kernel,
        grid=(HALF // 2,),
        out_shape=(half, shape(HALF, SEG), shape(NR, SEG, DIM, dtype=BF16)),
        in_specs=[smem()] + [vmem()] * 10,
        out_specs=(half_spec, vmem(), vmem()),
        compiler_params=params(32),
        cost_estimate=cost,
        name="first_affinity",
    )(position, first_columns, *pairs, four, across(four))
    second_block, degree = pl.pallas_call(
        second_kernel,
        grid=(HALF // 2,),
        out_shape=(half, shape(NC, NC, SEG)),
        in_specs=[smem()] + [vmem()] * 3,
        out_specs=(half_spec, vmem()),
        compiler_params=params(32),
        cost_estimate=cost,
        name="second_affinity",
    )(position, second_columns, rows, first_degree)
    degree = to_all(degree, COLS)
    mine, other, own = pl.pallas_call(
        apply_kernel,
        out_shape=(shape(HALF, VEC, SEG), shape(HALF, VEC, SEG), shape(1, SEG)),
        in_specs=[smem()] + [vmem()] * 3 + [pl.BlockSpec(memory_space=pl.ANY)] * 2,
        out_specs=(vmem(), vmem(), vmem()),
        scratch_shapes=[
            pltpu.VMEM((NC, SEG), F32),
            pltpu.VMEM((DEPTH, NR * SEG, SEG), BF16),
            pltpu.SemaphoreType.DMA((DEPTH,)),
        ],
        compiler_params=params(44),
        name="apply",
    )(position, degree, first_columns, second_columns, first_block, second_block)
    product = to_all(mine + across(other), "z")
    projected, gram = pl.pallas_call(
        project_kernel,
        out_shape=(shape(VEC, SEG), shape(2, 128)),
        name="project",
    )(product, own)
    gram = jnp.broadcast_to(gram + across(gram), (CHIPS, 2, 128))
    gram = to_all(gram, ("xl", "z", "y", "xh"))
    basis, triangle = pl.pallas_call(
        finish_kernel,
        out_shape=(shape(VEC, SEG), shape(VEC, VEC)),
        name="finish",
    )(gram, projected)
    return basis.T, triangle


def solution(mesh):
    torus = Mesh(mesh.devices.reshape(SIZES), AXES)
    placed = (P(AXES, None), P(AXES, None))
    return jax.shard_map(
        per_device, mesh=torus, in_specs=placed, out_specs=(P(AXES, None), P()), check_vma=False
    )
```

```python
import jax
import jax.numpy as jnp
from jax import lax
from jax.experimental import pallas as pl
from jax.experimental.pallas import tpu as pltpu
from jax.sharding import Mesh
from jax.sharding import PartitionSpec as P

AXES = ("xl", "z", "core", "y", "xh")
SIZES = (2, 8, 2, 4, 2)
ROWS = ("z", "core")
COLS = ("xl", "y", "xh")
CHIPS = 128
HALF = 8
NR = 16
NC = 16
SEG = 256
DIM = 192
VEC = 16
DEPTH = 6
SCALE = 14.426950408889634
UNSCALE = 4.5399929762484854e-05
EPS = 1e-6
NEAR = [(2 * k + j, chip, flip) for k, (chip, flip) in enumerate(((0, 0), (-1, 0), (1, 1), (-2, 0), (2, 1))) for j in range(2)]
FAR = [(2 * k + j, chip, flip) for k, (chip, flip) in enumerate(((-3, 0), (3, 1))) for j in range(2)]
MIB = 1 << 20
F32 = jnp.float32
BF16 = jnp.bfloat16
HI = lax.Precision.HIGHEST


def params(mib):
    return pltpu.CompilerParams(vmem_limit_bytes=mib * MIB)


def vmem():
    return pl.BlockSpec(memory_space=pltpu.VMEM)


def smem():
    return pl.BlockSpec(memory_space=pltpu.SMEM)


def nt(a, b, **kw):
    return lax.dot_general(a, b, (((1,), (1,)), ((), ())), preferred_element_type=F32, **kw)


def unit_kernel(e_ref, u_ref, many_ref):
    e = e_ref[...].astype(F32)
    u_ref[...] = (e * lax.rsqrt(jnp.sum(e * e, axis=0, keepdims=True) + EPS)).astype(BF16)
    for k in range(NC):
        many_ref[k] = u_ref[...]


def score_pieces(step, t_ref, s_ref, b_ref, keep):
    for j in range(2):
        t = step * 2 + j
        piece = t_ref[t]
        total = jnp.zeros((8, SEG), F32)
        for r in range(s_ref.shape[0]):
            score = jnp.dot(s_ref[r], piece, preferred_element_type=F32)
            tile = jnp.exp2(score * SCALE)
            total = total + jnp.sum(tile.reshape(SEG // 8, 8, SEG), axis=0)
            b_ref[j, r * SEG : (r + 1) * SEG, :] = tile.astype(BF16)
        keep(t, jnp.sum(total, axis=0, keepdims=True) * UNSCALE)


def near_kernel(t_ref, *refs):
    pairs = refs[0:5]
    b_ref, deg_ref, s_ref = refs[5:8]
    step = pl.program_id(0)

    @pl.when(step == 0)
    def _():
        for k in range(5):
            for j in range(2):
                s_ref[2 * k + j] = pairs[k][j].T

    def keep(t, sums):
        deg_ref[pl.ds(t, 1), :] = sums

    score_pieces(step, t_ref, s_ref, b_ref, keep)


def far_kernel(t_ref, near_deg_ref, v_ref, *refs):
    pairs, lone = refs[0:2], refs[2:4]
    b_ref, deg_ref, s_ref = refs[4:7]
    step = pl.program_id(0)

    @pl.when(step == 0)
    def _():
        for k in range(2):
            for j in range(2):
                s_ref[2 * k + j] = pairs[k][j].T
            s_ref[4 + k] = lone[k][...].T
        for k in range(NC):
            deg_ref[k, NC : NC + VEC, :] = v_ref[...]

    def keep(t, sums):
        sums = sums + near_deg_ref[pl.ds(t, 1), :]
        for k in range(NC):
            deg_ref[k, pl.ds(t, 1), :] = sums

    score_pieces(step, t_ref, s_ref, b_ref, keep)


def apply_kernel(pos_ref, deg_ref, near_ref, far_ref, *refs):
    mine_ref, other_ref, own_ref, root_ref, near_held, far_held, sem_ref = refs
    z, core = pos_ref[0], pos_ref[1]
    sign = 1 - 2 * core

    def fetch(t):
        slot = t % DEPTH
        return (
            pltpu.make_async_copy(near_ref.at[t], near_held.at[slot], sem_ref.at[0, slot]),
            pltpu.make_async_copy(far_ref.at[t], far_held.at[slot], sem_ref.at[1, slot]),
        )

    for t in range(DEPTH):
        for copy in fetch(t):
            copy.start()
    degree = deg_ref[0, 0:NC, :]
    for k in range(1, NC):
        degree = degree + deg_ref[k, 0:NC, :]
    root_ref[...] = lax.rsqrt(degree)
    own_ref[...] = root_ref[pl.ds(pos_ref[2], 1), :] * UNSCALE
    places = [(near_held, r, chip, r % 2 == flip) for r, chip, flip in NEAR]
    places += [(far_held, r, chip, r % 2 == flip) for r, chip, flip in FAR]
    places += [(far_held, 4, 4, True), (far_held, 5, 4, False)]
    for t in range(NC):
        w = (deg_ref[t, NC : NC + VEC, :] * root_ref[t : t + 1, :]).astype(BF16)
        for copy in fetch(t):
            copy.wait()
        for held, r, chip, same in places:
            part = nt(w, held[t % DEPTH, r * SEG : (r + 1) * SEG, :])
            p_ref = mine_ref if same else other_ref
            place = lax.rem(z + chip * sign + 16, 8)
            p_ref[place] = part if t == 0 else p_ref[place] + part
        if t + DEPTH < NC:
            for copy in fetch(t + DEPTH):
                copy.start()


def project_kernel(p_ref, own_ref, q_ref, gram_ref):
    q = jnp.sum(p_ref[...], axis=0) * own_ref[...]
    q_ref[...] = q
    down = jnp.concatenate([jnp.broadcast_to(q[a : a + 1], (VEC, SEG)) for a in range(VEC)], axis=0)
    pairs = down * jnp.concatenate([q] * VEC, axis=0)
    gram = nt(jnp.ones((8, SEG), F32), pairs, precision=HI)[0:1]
    flat = jnp.concatenate([gram[:, 0:128], gram[:, 128:256]], axis=0)
    gram_ref[...] = flat


def finish_kernel(gram_ref, q_ref, basis_ref, triangle_ref):
    flat = jnp.sum(gram_ref[...], axis=0)
    row = lax.broadcasted_iota(jnp.int32, (VEC, 128), 0)
    lane = lax.broadcasted_iota(jnp.int32, (VEC, 128), 1)
    low = jnp.where(lane // VEC == row, flat[0:1], 0.0)
    high = jnp.where(lane // VEC == row - 8, flat[1:2], 0.0)
    pick = jnp.where(
        lax.broadcasted_iota(jnp.int32, (128, 128), 0) % VEC
        == lax.broadcasted_iota(jnp.int32, (128, 128), 1),
        1.0,
        0.0,
    )
    g = jnp.dot(low + high, pick, preferred_element_type=F32, precision=HI)
    q = q_ref[...]
    wide = lax.broadcasted_iota(jnp.int32, (VEC, SEG), 0)
    for k in range(VEC):
        column = jnp.sum(jnp.where(lane == k, g, 0.0), axis=1, keepdims=True)
        inverse = lax.rsqrt(column[k : k + 1, :])
        factor = column * inverse
        top_g = g[k : k + 1, :] * inverse
        top_q = q[k : k + 1, :] * inverse
        g = jnp.where(row == k, top_g, jnp.where(row > k, g - factor * top_g, g))
        q = jnp.where(wide == k, top_q, jnp.where(wide > k, q - factor * top_q, q))
    basis_ref[...] = q
    triangle_ref[...] = jnp.where(lane >= row, g, 0.0)[:, 0:VEC]


def to_all(copies, axes):
    return lax.all_to_all(copies, axes, split_axis=0, concat_axis=0, tiled=True)


def shape(*dims, dtype=F32):
    return jax.ShapeDtypeStruct(dims, dtype)


def across(a):
    return lax.ppermute(a, "core", [(0, 1), (1, 0)])


def along(a, hops):
    turns = []
    for z in range(8):
        turns += [(z * 2, (z + hops) % 8 * 2), (z * 2 + 1, (z - hops) % 8 * 2 + 1)]
    return lax.ppermute(a, ROWS, turns)


def per_device(embeddings, vectors):
    position = jnp.stack([lax.axis_index("z"), lax.axis_index("core"), lax.axis_index(COLS)])
    unit, copies = pl.pallas_call(
        unit_kernel,
        out_shape=(shape(DIM, SEG, dtype=BF16), shape(NC, DIM, SEG, dtype=BF16)),
        name="unit",
    )(embeddings.T)
    columns = to_all(copies, COLS)
    pair = jnp.stack([unit, across(unit)])
    one, two = along(pair, 1), along(pair, 2)
    three, four = along(two, 1), along(two[0], 2)

    def affinity(kernel, name, count, operands, out_degree):
        return pl.pallas_call(
            kernel,
            grid=(NC // 2,),
            out_shape=(pltpu.HBM((NC, count * SEG, SEG), BF16), out_degree),
            in_specs=[vmem()] * len(operands),
            out_specs=(pl.BlockSpec((2, count * SEG, SEG), lambda i: (i, 0, 0)), vmem()),
            scratch_shapes=[pltpu.VMEM((count, SEG, DIM), BF16)],
            compiler_params=params(32),
            cost_estimate=pl.CostEstimate(
                flops=2 * 256 * 4096 * SEG * count,
                transcendentals=4096 * SEG * count,
                bytes_accessed=2 * 4096 * SEG * count,
            ),
            name=name,
        )(*operands)

    near = (columns, pair, one, across(one), two, across(two))
    near_block, near_degree = affinity(near_kernel, "near_affinity", 10, near, shape(NC, SEG))
    far = (columns, near_degree, vectors.T, three, across(three), four, across(four))
    far_block, degree = affinity(far_kernel, "far_affinity", 6, far, shape(NC, NC + VEC, SEG))
    degree = to_all(degree, COLS)
    mine, other, own = pl.pallas_call(
        apply_kernel,
        out_shape=(shape(HALF, VEC, SEG), shape(HALF, VEC, SEG), shape(1, SEG)),
        in_specs=[smem(), vmem()] + [pl.BlockSpec(memory_space=pl.ANY)] * 2,
        out_specs=(vmem(), vmem(), vmem()),
        scratch_shapes=[
            pltpu.VMEM((NC, SEG), F32),
            pltpu.VMEM((DEPTH, 10 * SEG, SEG), BF16),
            pltpu.VMEM((DEPTH, 6 * SEG, SEG), BF16),
            pltpu.SemaphoreType.DMA((2, DEPTH)),
        ],
        compiler_params=params(48),
        name="apply",
    )(position, degree, near_block, far_block)
    product = to_all(mine + across(other), "z")
    projected, gram = pl.pallas_call(
        project_kernel,
        out_shape=(shape(VEC, SEG), shape(2, 128)),
        name="project",
    )(product, own)
    gram = jnp.broadcast_to(gram + across(gram), (CHIPS, 2, 128))
    gram = to_all(gram, ("xl", "z", "y", "xh"))
    basis, triangle = pl.pallas_call(
        finish_kernel,
        out_shape=(shape(VEC, SEG), shape(VEC, VEC)),
        name="finish",
    )(gram, projected)
    return basis.T, triangle


def solution(mesh):
    torus = Mesh(mesh.devices.reshape(SIZES), AXES)
    placed = (P(AXES, None), P(AXES, None))
    return jax.shard_map(
        per_device, mesh=torus, in_specs=placed, out_specs=(P(AXES, None), P()), check_vma=False
    )
```

```python
import jax
import jax.numpy as jnp
from jax import lax
from jax.experimental import pallas as pl
from jax.experimental.pallas import tpu as pltpu
from jax.sharding import Mesh
from jax.sharding import PartitionSpec as P

AXES = ("xl", "z", "core", "y", "xh")
SIZES = (2, 8, 2, 4, 2)
ROWS = ("z", "core")
COLS = ("xl", "y", "xh")
CHIPS = 128
HALF = 8
NR = 16
NC = 16
SEG = 256
DIM = 192
VEC = 16
WIDE = DIM + 2 * VEC
DEPTH = 6
SCALE = 14.426950408889634
UNSCALE = 4.5399929762484854e-05
EPS = 1e-6
MIB = 1 << 20
F32 = jnp.float32
BF16 = jnp.bfloat16
HI = lax.Precision.HIGHEST


def params(mib):
    return pltpu.CompilerParams(vmem_limit_bytes=mib * MIB)


def vmem():
    return pl.BlockSpec(memory_space=pltpu.VMEM)


def smem():
    return pl.BlockSpec(memory_space=pltpu.SMEM)


def nt(a, b, **kw):
    return lax.dot_general(a, b, (((1,), (1,)), ((), ())), preferred_element_type=F32, **kw)


def unit_kernel(e_ref, v_ref, u_ref, many_ref):
    e = e_ref[...].astype(F32)
    u = (e * lax.rsqrt(jnp.sum(e * e, axis=0, keepdims=True) + EPS)).astype(BF16)
    u_ref[...] = u
    v = v_ref[...]
    high = v.astype(BF16)
    low = (v - high.astype(F32)).astype(BF16)
    for k in range(NC):
        many_ref[k, 0:DIM, :] = u
        many_ref[k, DIM : DIM + VEC, :] = high
        many_ref[k, DIM + VEC : WIDE, :] = low


def affinity_kernel(pos_ref, t_ref, *refs):
    pairs, lone = refs[0:7], refs[7:9]
    b_ref, deg_ref, s_ref = refs[9:12]
    z, core = pos_ref[0], pos_ref[1]
    step = pl.program_id(0)

    def place(chip, side, rows):
        s_ref[lax.rem(chip + 16, 8) * 2 + side] = rows.T

    @pl.when(step == 0)
    def _():
        sign = 1 - 2 * core
        place(z, core, pairs[0][0])
        place(z, 1 - core, pairs[0][1])
        for k in range(1, 4):
            place(z - k * sign, core, pairs[2 * k - 1][0])
            place(z - k * sign, 1 - core, pairs[2 * k - 1][1])
            place(z + k * sign, 1 - core, pairs[2 * k][0])
            place(z + k * sign, core, pairs[2 * k][1])
        place(z + 4, core, lone[0][...])
        place(z + 4, 1 - core, lone[1][...])

    for j in range(2):
        piece = t_ref[step * 2 + j, 0:DIM, :]
        total = jnp.zeros((8, SEG), F32)
        for r in range(NR):
            score = jnp.dot(s_ref[r], piece, preferred_element_type=F32)
            tile = jnp.exp2(score * SCALE)
            total = total + jnp.sum(tile.reshape(SEG // 8, 8, SEG), axis=0)
            b_ref[j, r * SEG : (r + 1) * SEG, :] = tile.astype(BF16)
        sums = jnp.sum(total, axis=0, keepdims=True) * UNSCALE
        for k in range(NC):
            deg_ref[k, pl.ds(step * 2 + j, 1), :] = sums


def apply_kernel(pos_ref, deg_ref, t_ref, b_ref, mine_ref, other_ref, own_ref, root_ref, held_ref, sem_ref):
    def fetch(t):
        slot = t % DEPTH
        return pltpu.make_async_copy(b_ref.at[t], held_ref.at[slot], sem_ref.at[slot])

    for t in range(DEPTH):
        fetch(t).start()
    root_ref[...] = lax.rsqrt(jnp.sum(deg_ref[...], axis=0))
    core = pos_ref[0]
    own_ref[...] = root_ref[pl.ds(pos_ref[1], 1), :] * UNSCALE
    for t in range(NC):
        v = t_ref[t, DIM : DIM + VEC, :].astype(F32) + t_ref[t, DIM + VEC : WIDE, :].astype(F32)
        w = (v * root_ref[t : t + 1, :]).astype(BF16)
        fetch(t).wait()
        for r in range(NR // 2):
            for side, p_ref in ((core, mine_ref), (1 - core, other_ref)):
                rows = pl.ds(pl.multiple_of((r * 2 + side) * SEG, SEG), SEG)
                part = nt(w, held_ref[t % DEPTH, rows, :])
                p_ref[r] = part if t == 0 else p_ref[r] + part
        if t + DEPTH < NC:
            fetch(t + DEPTH).start()


def project_kernel(p_ref, own_ref, q_ref, gram_ref):
    q = jnp.sum(p_ref[...], axis=0) * own_ref[...]
    q_ref[...] = q
    down = jnp.concatenate([jnp.broadcast_to(q[a : a + 1], (VEC, SEG)) for a in range(VEC)], axis=0)
    pairs = down * jnp.concatenate([q] * VEC, axis=0)
    gram = nt(jnp.ones((8, SEG), F32), pairs, precision=HI)[0:1]
    flat = jnp.concatenate([gram[:, 0:128], gram[:, 128:256]], axis=0)
    gram_ref[...] = flat


def finish_kernel(gram_ref, q_ref, basis_ref, triangle_ref):
    flat = jnp.sum(gram_ref[...], axis=0)
    row = lax.broadcasted_iota(jnp.int32, (VEC, 128), 0)
    lane = lax.broadcasted_iota(jnp.int32, (VEC, 128), 1)
    low = jnp.where(lane // VEC == row, flat[0:1], 0.0)
    high = jnp.where(lane // VEC == row - 8, flat[1:2], 0.0)
    pick = jnp.where(
        lax.broadcasted_iota(jnp.int32, (128, 128), 0) % VEC
        == lax.broadcasted_iota(jnp.int32, (128, 128), 1),
        1.0,
        0.0,
    )
    g = jnp.dot(low + high, pick, preferred_element_type=F32, precision=HI)
    q = q_ref[...]
    wide = lax.broadcasted_iota(jnp.int32, (VEC, SEG), 0)
    for k in range(VEC):
        column = jnp.sum(jnp.where(lane == k, g, 0.0), axis=1, keepdims=True)
        inverse = lax.rsqrt(column[k : k + 1, :])
        factor = column * inverse
        top_g = g[k : k + 1, :] * inverse
        top_q = q[k : k + 1, :] * inverse
        g = jnp.where(row == k, top_g, jnp.where(row > k, g - factor * top_g, g))
        q = jnp.where(wide == k, top_q, jnp.where(wide > k, q - factor * top_q, q))
    basis_ref[...] = q
    triangle_ref[...] = jnp.where(lane >= row, g, 0.0)[:, 0:VEC]


def to_all(copies, axes):
    return lax.all_to_all(copies, axes, split_axis=0, concat_axis=0, tiled=True)


def shape(*dims, dtype=F32):
    return jax.ShapeDtypeStruct(dims, dtype)


def across(a):
    return lax.ppermute(a, "core", [(0, 1), (1, 0)])


def along(a, hops):
    turns = []
    for z in range(8):
        turns += [(z * 2, (z + hops) % 8 * 2), (z * 2 + 1, (z - hops) % 8 * 2 + 1)]
    return lax.ppermute(a, ROWS, turns)


def per_device(embeddings, vectors):
    z, core = lax.axis_index("z"), lax.axis_index("core")
    column = lax.axis_index(COLS)
    unit, unit_copies = pl.pallas_call(
        unit_kernel,
        out_shape=(shape(DIM, SEG, dtype=BF16), shape(NC, WIDE, SEG, dtype=BF16)),
        name="unit",
    )(embeddings.T, vectors.T)
    columns = to_all(unit_copies, COLS)
    pair = jnp.stack([unit, across(unit)])
    one, two = along(pair, 1), along(pair, 2)
    three, four = along(two, 1), along(two[0], 2)
    pairs = (pair, one, across(one), two, across(two), three, across(three))
    block, degree = pl.pallas_call(
        affinity_kernel,
        grid=(NC // 2,),
        out_shape=(shape(NC, NR * SEG, SEG, dtype=BF16), shape(NC, NC, SEG)),
        in_specs=[smem()] + [vmem()] * 10,
        out_specs=(pl.BlockSpec((2, NR * SEG, SEG), lambda i: (i, 0, 0)), vmem()),
        scratch_shapes=[pltpu.VMEM((NR, SEG, DIM), BF16)],
        compiler_params=params(32),
        cost_estimate=pl.CostEstimate(
            flops=2 * 256 * 4096 * 4096, transcendentals=4096 * 4096, bytes_accessed=1 << 25
        ),
        name="affinity",
    )(jnp.stack([z, core]), columns, *pairs, four, across(four))
    degree = to_all(degree, COLS)
    mine, other, own = pl.pallas_call(
        apply_kernel,
        out_shape=(shape(HALF, VEC, SEG), shape(HALF, VEC, SEG), shape(1, SEG)),
        in_specs=[smem(), vmem(), vmem(), pl.BlockSpec(memory_space=pl.ANY)],
        out_specs=(vmem(), vmem(), vmem()),
        scratch_shapes=[
            pltpu.VMEM((NC, SEG), F32),
            pltpu.VMEM((DEPTH, NR * SEG, SEG), BF16),
            pltpu.SemaphoreType.DMA((DEPTH,)),
        ],
        compiler_params=params(44),
        name="apply",
    )(jnp.stack([core, column]), degree, columns, block)
    product = to_all(mine + across(other), "z")
    projected, gram = pl.pallas_call(
        project_kernel,
        out_shape=(shape(VEC, SEG), shape(2, 128)),
        name="project",
    )(product, own)
    gram = jnp.broadcast_to(gram + across(gram), (CHIPS, 2, 128))
    gram = to_all(gram, ("xl", "z", "y", "xh"))
    basis, triangle = pl.pallas_call(
        finish_kernel,
        out_shape=(shape(VEC, SEG), shape(VEC, VEC)),
        name="finish",
    )(gram, projected)
    return basis.T, triangle


def solution(mesh):
    torus = Mesh(mesh.devices.reshape(SIZES), AXES)
    placed = (P(AXES, None), P(AXES, None))
    return jax.shard_map(
        per_device, mesh=torus, in_specs=placed, out_specs=(P(AXES, None), P()), check_vma=False
    )
```

```python
import jax
import jax.numpy as jnp
from jax import lax
from jax.experimental import pallas as pl
from jax.experimental.pallas import tpu as pltpu
from jax.sharding import Mesh
from jax.sharding import PartitionSpec as P

AXES = ("xl", "z", "core", "y", "xh")
SIZES = (2, 8, 2, 4, 2)
ROWS = ("z", "core")
COLS = ("xl", "y", "xh")
CHIPS = 128
HALF = 8
KEPT = 13
NR = 16
NC = 16
SEG = 256
DIM = 192
VEC = 16
WIDE = DIM + 2 * VEC
DEPTH = 6
SCALE = 14.426950408889634
UNSCALE = 4.5399929762484854e-05
EPS = 1e-6
SLOTS = [(0, True), (0, False)]
for _hops in (1, 2, 3):
    SLOTS += [(-_hops, True), (-_hops, False), (_hops, False), (_hops, True)]
SLOTS += [(4, True), (4, False)]
MIB = 1 << 20
F32 = jnp.float32
BF16 = jnp.bfloat16
HI = lax.Precision.HIGHEST


def params(mib):
    return pltpu.CompilerParams(vmem_limit_bytes=mib * MIB)


def vmem():
    return pl.BlockSpec(memory_space=pltpu.VMEM)


def smem():
    return pl.BlockSpec(memory_space=pltpu.SMEM)


def nt(a, b, **kw):
    return lax.dot_general(a, b, (((1,), (1,)), ((), ())), preferred_element_type=F32, **kw)


def unit_kernel(e_ref, v_ref, u_ref, many_ref):
    e = e_ref[...].astype(F32)
    u = (e * lax.rsqrt(jnp.sum(e * e, axis=0, keepdims=True) + EPS)).astype(BF16)
    u_ref[...] = u
    v = v_ref[...]
    high = v.astype(BF16)
    low = (v - high.astype(F32)).astype(BF16)
    for k in range(NC):
        many_ref[k, 0:DIM, :] = u
        many_ref[k, DIM : DIM + VEC, :] = high
        many_ref[k, DIM + VEC : WIDE, :] = low


def turn_kernel(*refs):
    pairs, lone, rows_ref = refs[0:7], refs[7:9], refs[9]
    for k in range(7):
        for j in range(2):
            rows_ref[2 * k + j] = pairs[k][j].T
    for k in range(2):
        rows_ref[14 + k] = lone[k][...].T


def affinity_kernel(t_ref, s_ref, b_ref, deg_ref):
    step = pl.program_id(0)

    def score_piece(keep):
        piece = t_ref[step, 0:DIM, :]
        total = jnp.zeros((8, SEG), F32)
        for r in range(NR):
            score = jnp.dot(s_ref[r], piece, preferred_element_type=F32)
            tile = jnp.exp2(score * SCALE)
            total = total + jnp.sum(tile.reshape(SEG // 8, 8, SEG), axis=0)
            if keep:
                b_ref[0, r * SEG : (r + 1) * SEG, :] = tile.astype(BF16)
        sums = jnp.sum(total, axis=0, keepdims=True) * UNSCALE
        for k in range(NC):
            deg_ref[k, pl.ds(step, 1), :] = sums

    pl.when(step < KEPT)(lambda: score_piece(True))
    pl.when(step >= KEPT)(lambda: score_piece(False))


def apply_kernel(pos_ref, deg_ref, t_ref, s_ref, b_ref, *refs):
    mine_ref, other_ref, own_ref, root_ref, held_ref, sem_ref = refs
    z, core = pos_ref[0], pos_ref[1]
    sign = 1 - 2 * core

    def fetch(t):
        slot = t % DEPTH
        return pltpu.make_async_copy(b_ref.at[t], held_ref.at[slot], sem_ref.at[slot])

    for t in range(DEPTH):
        fetch(t).start()
    root_ref[...] = lax.rsqrt(jnp.sum(deg_ref[...], axis=0))
    own_ref[...] = root_ref[pl.ds(pos_ref[2], 1), :] * UNSCALE
    mine_ref[...] = jnp.zeros_like(mine_ref)
    other_ref[...] = jnp.zeros_like(other_ref)

    def column_piece(t, tile_of):
        v = t_ref[t, DIM : DIM + VEC, :].astype(F32) + t_ref[t, DIM + VEC : WIDE, :].astype(F32)
        w = (v * root_ref[t : t + 1, :]).astype(BF16)
        for r, (chip, same) in enumerate(SLOTS):
            p_ref = mine_ref if same else other_ref
            place = lax.rem(z + chip * sign + 16, 8)
            p_ref[place] = p_ref[place] + nt(w, tile_of(r))

    for t in range(KEPT, NC):

        def again(r):
            score = jnp.dot(s_ref[r], t_ref[t, 0:DIM, :], preferred_element_type=F32)
            return jnp.exp2(score * SCALE).astype(BF16)

        column_piece(t, again)
    for t in range(KEPT):
        fetch(t).wait()
        column_piece(t, lambda r: held_ref[t % DEPTH, r * SEG : (r + 1) * SEG, :])
        if t + DEPTH < KEPT:
            fetch(t + DEPTH).start()


def project_kernel(p_ref, own_ref, q_ref, gram_ref):
    q = jnp.sum(p_ref[...], axis=0) * own_ref[...]
    q_ref[...] = q
    down = jnp.concatenate([jnp.broadcast_to(q[a : a + 1], (VEC, SEG)) for a in range(VEC)], axis=0)
    pairs = down * jnp.concatenate([q] * VEC, axis=0)
    gram = nt(jnp.ones((8, SEG), F32), pairs, precision=HI)[0:1]
    flat = jnp.concatenate([gram[:, 0:128], gram[:, 128:256]], axis=0)
    gram_ref[...] = flat


def finish_kernel(gram_ref, q_ref, basis_ref, triangle_ref):
    flat = jnp.sum(gram_ref[...], axis=0)
    row = lax.broadcasted_iota(jnp.int32, (VEC, 128), 0)
    lane = lax.broadcasted_iota(jnp.int32, (VEC, 128), 1)
    low = jnp.where(lane // VEC == row, flat[0:1], 0.0)
    high = jnp.where(lane // VEC == row - 8, flat[1:2], 0.0)
    pick = jnp.where(
        lax.broadcasted_iota(jnp.int32, (128, 128), 0) % VEC
        == lax.broadcasted_iota(jnp.int32, (128, 128), 1),
        1.0,
        0.0,
    )
    g = jnp.dot(low + high, pick, preferred_element_type=F32, precision=HI)
    q = q_ref[...]
    wide = lax.broadcasted_iota(jnp.int32, (VEC, SEG), 0)
    for k in range(VEC):
        column = jnp.sum(jnp.where(lane == k, g, 0.0), axis=1, keepdims=True)
        inverse = lax.rsqrt(column[k : k + 1, :])
        factor = column * inverse
        top_g = g[k : k + 1, :] * inverse
        top_q = q[k : k + 1, :] * inverse
        g = jnp.where(row == k, top_g, jnp.where(row > k, g - factor * top_g, g))
        q = jnp.where(wide == k, top_q, jnp.where(wide > k, q - factor * top_q, q))
    basis_ref[...] = q
    triangle_ref[...] = jnp.where(lane >= row, g, 0.0)[:, 0:VEC]


def to_all(copies, axes):
    return lax.all_to_all(copies, axes, split_axis=0, concat_axis=0, tiled=True)


def shape(*dims, dtype=F32):
    return jax.ShapeDtypeStruct(dims, dtype)


def across(a):
    return lax.ppermute(a, "core", [(0, 1), (1, 0)])


def along(a, hops):
    turns = []
    for z in range(8):
        turns += [(z * 2, (z + hops) % 8 * 2), (z * 2 + 1, (z - hops) % 8 * 2 + 1)]
    return lax.ppermute(a, ROWS, turns)


def per_device(embeddings, vectors):
    z, core = lax.axis_index("z"), lax.axis_index("core")
    column = lax.axis_index(COLS)
    unit, unit_copies = pl.pallas_call(
        unit_kernel,
        out_shape=(shape(DIM, SEG, dtype=BF16), shape(NC, WIDE, SEG, dtype=BF16)),
        compiler_params=params(8),
        name="unit",
    )(embeddings.T, vectors.T)
    columns = to_all(unit_copies, COLS)
    pair = jnp.stack([unit, across(unit)])
    one, two = along(pair, 1), along(pair, 2)
    three, four = along(two, 1), along(two[0], 2)
    pairs = (pair, one, across(one), two, across(two), three, across(three))
    rows = pl.pallas_call(
        turn_kernel,
        out_shape=shape(NR, SEG, DIM, dtype=BF16),
        compiler_params=params(8),
        name="turn",
    )(*pairs, four, across(four))
    block, degree = pl.pallas_call(
        affinity_kernel,
        grid=(NC,),
        out_shape=(pltpu.HBM((KEPT, NR * SEG, SEG), BF16), shape(NC, NC, SEG)),
        in_specs=[vmem()] * 2,
        out_specs=(
            pl.BlockSpec((1, NR * SEG, SEG), lambda i: (jnp.minimum(i, KEPT - 1), 0, 0)),
            vmem(),
        ),
        compiler_params=params(32),
        cost_estimate=pl.CostEstimate(
            flops=2 * 256 * 4096 * 4096, transcendentals=4096 * 4096, bytes_accessed=1 << 25
        ),
        name="affinity",
    )(columns, rows)
    degree = to_all(degree, COLS)
    mine, other, own = pl.pallas_call(
        apply_kernel,
        out_shape=(shape(HALF, VEC, SEG), shape(HALF, VEC, SEG), shape(1, SEG)),
        in_specs=[smem()] + [vmem()] * 3 + [pl.BlockSpec(memory_space=pl.ANY)],
        out_specs=(vmem(), vmem(), vmem()),
        scratch_shapes=[
            pltpu.VMEM((NC, SEG), F32),
            pltpu.VMEM((DEPTH, NR * SEG, SEG), BF16),
            pltpu.SemaphoreType.DMA((DEPTH,)),
        ],
        compiler_params=params(44),
        name="apply",
    )(jnp.stack([z, core, column]), degree, columns, rows, block)
    product = to_all(mine + across(other), "z")
    projected, gram = pl.pallas_call(
        project_kernel,
        out_shape=(shape(VEC, SEG), shape(2, 128)),
        compiler_params=params(8),
        name="project",
    )(product, own)
    gram = jnp.broadcast_to(gram + across(gram), (CHIPS, 2, 128))
    gram = to_all(gram, ("xl", "z", "y", "xh"))
    basis, triangle = pl.pallas_call(
        finish_kernel,
        out_shape=(shape(VEC, SEG), shape(VEC, VEC)),
        compiler_params=params(8),
        name="finish",
    )(gram, projected)
    return basis.T, triangle


def solution(mesh):
    torus = Mesh(mesh.devices.reshape(SIZES), AXES)
    placed = (P(AXES, None), P(AXES, None))
    return jax.shard_map(
        per_device, mesh=torus, in_specs=placed, out_specs=(P(AXES, None), P()), check_vma=False
    )
```

```python
import jax
import jax.numpy as jnp
from jax import lax
from jax.experimental import pallas as pl
from jax.experimental.pallas import tpu as pltpu
from jax.sharding import Mesh
from jax.sharding import PartitionSpec as P

AXES = ("xl", "z", "core", "y", "xh")
SIZES = (2, 8, 2, 4, 2)
ROWS = ("z", "core")
COLS = ("xl", "y", "xh")
CHIPS = 128
HALF = 8
KEPT = 14
NR = 16
NC = 16
SEG = 256
DIM = 192
VEC = 16
WIDE = DIM + 2 * VEC
DEPTH = 6
SCALE = 14.426950408889634
UNSCALE = 4.5399929762484854e-05
EPS = 1e-6
SLOTS = [(0, True), (0, False)]
for _hops in (1, 2, 3):
    SLOTS += [(-_hops, True), (-_hops, False), (_hops, False), (_hops, True)]
SLOTS += [(4, True), (4, False)]
MIB = 1 << 20
F32 = jnp.float32
BF16 = jnp.bfloat16
HI = lax.Precision.HIGHEST


def params(mib):
    return pltpu.CompilerParams(vmem_limit_bytes=mib * MIB)


def vmem():
    return pl.BlockSpec(memory_space=pltpu.VMEM)


def smem():
    return pl.BlockSpec(memory_space=pltpu.SMEM)


def nt(a, b, **kw):
    return lax.dot_general(a, b, (((1,), (1,)), ((), ())), preferred_element_type=F32, **kw)


def unit_kernel(e_ref, v_ref, u_ref, many_ref):
    e = e_ref[...].astype(F32)
    u = (e * lax.rsqrt(jnp.sum(e * e, axis=0, keepdims=True) + EPS)).astype(BF16)
    u_ref[...] = u
    v = v_ref[...]
    high = v.astype(BF16)
    low = (v - high.astype(F32)).astype(BF16)
    for k in range(NC):
        many_ref[k, 0:DIM, :] = u
        many_ref[k, DIM : DIM + VEC, :] = high
        many_ref[k, DIM + VEC : WIDE, :] = low


def turn_kernel(*refs):
    pairs, lone, rows_ref = refs[0:7], refs[7:9], refs[9]
    for k in range(7):
        for j in range(2):
            rows_ref[2 * k + j] = pairs[k][j].T
    for k in range(2):
        rows_ref[14 + k] = lone[k][...].T


def affinity_kernel(t_ref, s_ref, b_ref, deg_ref):
    step = pl.program_id(0)

    def score_pieces(keep):
        for j in range(2):
            t = step * 2 + j
            piece = t_ref[t, 0:DIM, :]
            total = jnp.zeros((8, SEG), F32)
            for r in range(NR):
                score = jnp.dot(s_ref[r], piece, preferred_element_type=F32)
                tile = jnp.exp2(score * SCALE)
                total = total + jnp.sum(tile.reshape(SEG // 8, 8, SEG), axis=0)
                if keep:
                    b_ref[j, r * SEG : (r + 1) * SEG, :] = tile.astype(BF16)
            sums = jnp.sum(total, axis=0, keepdims=True) * UNSCALE
            for k in range(NC):
                deg_ref[k, pl.ds(t, 1), :] = sums

    if KEPT == NC:
        score_pieces(True)
    else:
        pl.when(step < KEPT // 2)(lambda: score_pieces(True))
        pl.when(step >= KEPT // 2)(lambda: score_pieces(False))


def apply_kernel(pos_ref, deg_ref, t_ref, s_ref, b_ref, *refs):
    mine_ref, other_ref, own_ref, root_ref, held_ref, acc_ref, sem_ref = refs
    z, core = pos_ref[0], pos_ref[1]
    sign = 1 - 2 * core

    def fetch(t):
        slot = t % DEPTH
        return pltpu.make_async_copy(b_ref.at[t], held_ref.at[slot], sem_ref.at[slot])

    for t in range(DEPTH):
        fetch(t).start()
    root_ref[...] = lax.rsqrt(jnp.sum(deg_ref[...], axis=0))
    own_ref[...] = root_ref[pl.ds(pos_ref[2], 1), :] * UNSCALE

    def column_piece(t, first, tile_of):
        v = t_ref[t, DIM : DIM + VEC, :].astype(F32) + t_ref[t, DIM + VEC : WIDE, :].astype(F32)
        w = (v * root_ref[t : t + 1, :]).astype(BF16)
        for r in range(NR):
            part = nt(w, tile_of(r))
            acc_ref[r] = part if first else acc_ref[r] + part

    for t in range(KEPT, NC):

        def again(r):
            score = jnp.dot(s_ref[r], t_ref[t, 0:DIM, :], preferred_element_type=F32)
            return jnp.exp2(score * SCALE).astype(BF16)

        column_piece(t, t == KEPT, again)
    for t in range(KEPT):
        fetch(t).wait()
        column_piece(
            t,
            KEPT == NC and t == 0,
            lambda r: held_ref[t % DEPTH, r * SEG : (r + 1) * SEG, :],
        )
        if t + DEPTH < KEPT:
            fetch(t + DEPTH).start()
    for r, (chip, same) in enumerate(SLOTS):
        p_ref = mine_ref if same else other_ref
        p_ref[lax.rem(z + chip * sign + 16, 8)] = acc_ref[r]


def project_kernel(p_ref, own_ref, q_ref, gram_ref):
    q = jnp.sum(p_ref[...], axis=0) * own_ref[...]
    q_ref[...] = q
    down = jnp.concatenate([jnp.broadcast_to(q[a : a + 1], (VEC, SEG)) for a in range(VEC)], axis=0)
    pairs = down * jnp.concatenate([q] * VEC, axis=0)
    gram = nt(jnp.ones((8, SEG), F32), pairs, precision=HI)[0:1]
    flat = jnp.concatenate([gram[:, 0:128], gram[:, 128:256]], axis=0)
    gram_ref[...] = flat


def finish_kernel(gram_ref, q_ref, basis_ref, triangle_ref):
    flat = jnp.sum(gram_ref[...], axis=0)
    row = lax.broadcasted_iota(jnp.int32, (VEC, 128), 0)
    lane = lax.broadcasted_iota(jnp.int32, (VEC, 128), 1)
    low = jnp.where(lane // VEC == row, flat[0:1], 0.0)
    high = jnp.where(lane // VEC == row - 8, flat[1:2], 0.0)
    pick = jnp.where(
        lax.broadcasted_iota(jnp.int32, (128, 128), 0) % VEC
        == lax.broadcasted_iota(jnp.int32, (128, 128), 1),
        1.0,
        0.0,
    )
    g = jnp.dot(low + high, pick, preferred_element_type=F32, precision=HI)
    q = q_ref[...]
    wide = lax.broadcasted_iota(jnp.int32, (VEC, SEG), 0)
    for k in range(VEC):
        column = jnp.sum(jnp.where(lane == k, g, 0.0), axis=1, keepdims=True)
        inverse = lax.rsqrt(column[k : k + 1, :])
        factor = column * inverse
        top_g = g[k : k + 1, :] * inverse
        top_q = q[k : k + 1, :] * inverse
        g = jnp.where(row == k, top_g, jnp.where(row > k, g - factor * top_g, g))
        q = jnp.where(wide == k, top_q, jnp.where(wide > k, q - factor * top_q, q))
    basis_ref[...] = q
    triangle_ref[...] = jnp.where(lane >= row, g, 0.0)[:, 0:VEC]


def to_all(copies, axes):
    return lax.all_to_all(copies, axes, split_axis=0, concat_axis=0, tiled=True)


def shape(*dims, dtype=F32):
    return jax.ShapeDtypeStruct(dims, dtype)


def across(a):
    return lax.ppermute(a, "core", [(0, 1), (1, 0)])


def along(a, hops):
    turns = []
    for z in range(8):
        turns += [(z * 2, (z + hops) % 8 * 2), (z * 2 + 1, (z - hops) % 8 * 2 + 1)]
    return lax.ppermute(a, ROWS, turns)


def per_device(embeddings, vectors):
    z, core = lax.axis_index("z"), lax.axis_index("core")
    column = lax.axis_index(COLS)
    unit, unit_copies = pl.pallas_call(
        unit_kernel,
        out_shape=(shape(DIM, SEG, dtype=BF16), shape(NC, WIDE, SEG, dtype=BF16)),
        name="unit",
    )(embeddings.T, vectors.T)
    columns = to_all(unit_copies, COLS)
    pair = jnp.stack([unit, across(unit)])
    one, two = along(pair, 1), along(pair, 2)
    three, four = along(two, 1), along(two[0], 2)
    pairs = (pair, one, across(one), two, across(two), three, across(three))
    rows = pl.pallas_call(
        turn_kernel,
        out_shape=shape(NR, SEG, DIM, dtype=BF16),
        compiler_params=params(8),
        name="turn",
    )(*pairs, four, across(four))
    block, degree = pl.pallas_call(
        affinity_kernel,
        grid=(NC // 2,),
        out_shape=(pltpu.HBM((KEPT, NR * SEG, SEG), BF16), shape(NC, NC, SEG)),
        in_specs=[vmem()] * 2,
        out_specs=(
            pl.BlockSpec((2, NR * SEG, SEG), lambda i: (jnp.minimum(i, KEPT // 2 - 1), 0, 0)),
            vmem(),
        ),
        compiler_params=params(32),
        cost_estimate=pl.CostEstimate(
            flops=2 * 256 * 4096 * 4096, transcendentals=4096 * 4096, bytes_accessed=1 << 25
        ),
        name="affinity",
    )(columns, rows)
    degree = to_all(degree, COLS)
    mine, other, own = pl.pallas_call(
        apply_kernel,
        out_shape=(shape(HALF, VEC, SEG), shape(HALF, VEC, SEG), shape(1, SEG)),
        in_specs=[smem()] + [vmem()] * 3 + [pl.BlockSpec(memory_space=pl.ANY)],
        out_specs=(vmem(), vmem(), vmem()),
        scratch_shapes=[
            pltpu.VMEM((NC, SEG), F32),
            pltpu.VMEM((DEPTH, NR * SEG, SEG), BF16),
            pltpu.VMEM((NR, VEC, SEG), F32),
            pltpu.SemaphoreType.DMA((DEPTH,)),
        ],
        compiler_params=params(44),
        name="apply",
    )(jnp.stack([z, core, column]), degree, columns, rows, block)
    product = to_all(mine + across(other), "z")
    projected, gram = pl.pallas_call(
        project_kernel,
        out_shape=(shape(VEC, SEG), shape(2, 128)),
        compiler_params=params(8),
        name="project",
    )(product, own)
    gram = jnp.broadcast_to(gram + across(gram), (CHIPS, 2, 128))
    gram = to_all(gram, ("xl", "z", "y", "xh"))
    basis, triangle = pl.pallas_call(
        finish_kernel,
        out_shape=(shape(VEC, SEG), shape(VEC, VEC)),
        compiler_params=params(8),
        name="finish",
    )(gram, projected)
    return basis.T, triangle


def solution(mesh):
    torus = Mesh(mesh.devices.reshape(SIZES), AXES)
    placed = (P(AXES, None), P(AXES, None))
    return jax.shard_map(
        per_device, mesh=torus, in_specs=placed, out_specs=(P(AXES, None), P()), check_vma=False
    )
```

```python
import jax
import jax.numpy as jnp
from jax import lax
from jax.experimental import pallas as pl
from jax.experimental.pallas import tpu as pltpu
from jax.sharding import Mesh
from jax.sharding import PartitionSpec as P

AXES = ("xl", "z", "core", "y", "xh")
SIZES = (2, 8, 2, 4, 2)
ROWS = ("z", "core")
COLS = ("xl", "y", "xh")
CHIPS = 128
HALF = 8
NR = 16
NC = 16
SEG = 256
DIM = 192
VEC = 16
WIDE = DIM + 2 * VEC
DEPTH = 6
SCALE = 14.426950408889634
UNSCALE = 4.5399929762484854e-05
EPS = 1e-6
MIB = 1 << 20
F32 = jnp.float32
BF16 = jnp.bfloat16
HI = lax.Precision.HIGHEST


def params(mib):
    return pltpu.CompilerParams(vmem_limit_bytes=mib * MIB)


def vmem():
    return pl.BlockSpec(memory_space=pltpu.VMEM)


def smem():
    return pl.BlockSpec(memory_space=pltpu.SMEM)


def nt(a, b, **kw):
    return lax.dot_general(a, b, (((1,), (1,)), ((), ())), preferred_element_type=F32, **kw)


def unit_kernel(e_ref, v_ref, u_ref, many_ref):
    e = e_ref[...].astype(F32)
    u = (e * lax.rsqrt(jnp.sum(e * e, axis=0, keepdims=True) + EPS)).astype(BF16)
    u_ref[...] = u
    v = v_ref[...]
    high = v.astype(BF16)
    low = (v - high.astype(F32)).astype(BF16)
    for k in range(NC):
        many_ref[k, 0:DIM, :] = u
        many_ref[k, DIM : DIM + VEC, :] = high
        many_ref[k, DIM + VEC : WIDE, :] = low


def affinity_kernel(pos_ref, t_ref, *refs):
    pairs, lone = refs[0:7], refs[7:9]
    b_ref, deg_ref, s_ref = refs[9:12]
    z, core = pos_ref[0], pos_ref[1]
    step = pl.program_id(0)

    def place(chip, side, rows):
        s_ref[lax.rem(chip + 16, 8) * 2 + side] = rows.T

    @pl.when(step == 0)
    def _():
        sign = 1 - 2 * core
        place(z, core, pairs[0][0])
        place(z, 1 - core, pairs[0][1])
        for k in range(1, 4):
            place(z - k * sign, core, pairs[2 * k - 1][0])
            place(z - k * sign, 1 - core, pairs[2 * k - 1][1])
            place(z + k * sign, 1 - core, pairs[2 * k][0])
            place(z + k * sign, core, pairs[2 * k][1])
        place(z + 4, core, lone[0][...])
        place(z + 4, 1 - core, lone[1][...])

    for j in range(2):
        piece = t_ref[step * 2 + j, 0:DIM, :]
        total = jnp.zeros((8, SEG), F32)
        for r in range(NR):
            score = jnp.dot(s_ref[r], piece, preferred_element_type=F32)
            tile = jnp.exp2(score * SCALE)
            total = total + jnp.sum(tile.reshape(SEG // 8, 8, SEG), axis=0)
            b_ref[j, r * SEG : (r + 1) * SEG, :] = tile.astype(BF16)
        sums = jnp.sum(total, axis=0, keepdims=True) * UNSCALE
        for k in range(NC):
            deg_ref[k, pl.ds(step * 2 + j, 1), :] = sums


def apply_kernel(pos_ref, deg_ref, t_ref, b_ref, mine_ref, other_ref, own_ref, root_ref, held_ref, sem_ref):
    def fetch(t):
        slot = t % DEPTH
        return pltpu.make_async_copy(b_ref.at[t], held_ref.at[slot], sem_ref.at[slot])

    for t in range(DEPTH):
        fetch(t).start()
    root_ref[...] = lax.rsqrt(jnp.sum(deg_ref[...], axis=0))
    core = pos_ref[0]
    own_ref[...] = root_ref[pl.ds(pos_ref[1], 1), :] * UNSCALE
    for t in range(NC):
        v = t_ref[t, DIM : DIM + VEC, :].astype(F32) + t_ref[t, DIM + VEC : WIDE, :].astype(F32)
        w = (v * root_ref[t : t + 1, :]).astype(BF16)
        fetch(t).wait()
        for r in range(NR // 2):
            for side, p_ref in ((core, mine_ref), (1 - core, other_ref)):
                rows = pl.ds(pl.multiple_of((r * 2 + side) * SEG, SEG), SEG)
                part = nt(w, held_ref[t % DEPTH, rows, :])
                p_ref[r] = part if t == 0 else p_ref[r] + part
        if t + DEPTH < NC:
            fetch(t + DEPTH).start()


def project_kernel(p_ref, own_ref, q_ref, gram_ref):
    q = jnp.sum(p_ref[...], axis=0) * own_ref[...]
    q_ref[...] = q
    down = jnp.concatenate([jnp.broadcast_to(q[a : a + 1], (VEC, SEG)) for a in range(VEC)], axis=0)
    pairs = down * jnp.concatenate([q] * VEC, axis=0)
    gram = nt(jnp.ones((8, SEG), F32), pairs, precision=HI)[0:1]
    flat = jnp.concatenate([gram[:, 0:128], gram[:, 128:256]], axis=0)
    gram_ref[...] = flat


def finish_kernel(gram_ref, q_ref, basis_ref, triangle_ref):
    flat = jnp.sum(gram_ref[...], axis=0)
    row = lax.broadcasted_iota(jnp.int32, (VEC, 128), 0)
    lane = lax.broadcasted_iota(jnp.int32, (VEC, 128), 1)
    low = jnp.where(lane // VEC == row, flat[0:1], 0.0)
    high = jnp.where(lane // VEC == row - 8, flat[1:2], 0.0)
    pick = jnp.where(
        lax.broadcasted_iota(jnp.int32, (128, 128), 0) % VEC
        == lax.broadcasted_iota(jnp.int32, (128, 128), 1),
        1.0,
        0.0,
    )
    g = jnp.dot(low + high, pick, preferred_element_type=F32, precision=HI)
    q = q_ref[...]
    wide = lax.broadcasted_iota(jnp.int32, (VEC, SEG), 0)
    for k in range(VEC):
        column = jnp.sum(jnp.where(lane == k, g, 0.0), axis=1, keepdims=True)
        inverse = lax.rsqrt(column[k : k + 1, :])
        factor = column * inverse
        top_g = g[k : k + 1, :] * inverse
        top_q = q[k : k + 1, :] * inverse
        g = jnp.where(row == k, top_g, jnp.where(row > k, g - factor * top_g, g))
        q = jnp.where(wide == k, top_q, jnp.where(wide > k, q - factor * top_q, q))
    basis_ref[...] = q
    triangle_ref[...] = jnp.where(lane >= row, g, 0.0)[:, 0:VEC]


def to_all(copies, axes):
    return lax.all_to_all(copies, axes, split_axis=0, concat_axis=0, tiled=True)


def shape(*dims, dtype=F32):
    return jax.ShapeDtypeStruct(dims, dtype)


def across(a):
    return lax.ppermute(a, "core", [(0, 1), (1, 0)])


def along(a, hops):
    turns = []
    for z in range(8):
        turns += [(z * 2, (z + hops) % 8 * 2), (z * 2 + 1, (z - hops) % 8 * 2 + 1)]
    return lax.ppermute(a, ROWS, turns)


def per_device(embeddings, vectors):
    z, core = lax.axis_index("z"), lax.axis_index("core")
    column = lax.axis_index(COLS)
    unit, unit_copies = pl.pallas_call(
        unit_kernel,
        out_shape=(shape(DIM, SEG, dtype=BF16), shape(NC, WIDE, SEG, dtype=BF16)),
        name="unit",
    )(embeddings.T, vectors.T)
    columns = to_all(unit_copies, COLS)
    pair = jnp.stack([unit, across(unit)])
    one, two = along(pair, 1), along(pair, 2)
    three, four = along(two, 1), along(two[0], 2)
    pairs = (pair, one, across(one), two, across(two), three, across(three))
    block, degree = pl.pallas_call(
        affinity_kernel,
        grid=(NC // 2,),
        out_shape=(shape(NC, NR * SEG, SEG, dtype=BF16), shape(NC, NC, SEG)),
        in_specs=[smem()] + [vmem()] * 10,
        out_specs=(pl.BlockSpec((2, NR * SEG, SEG), lambda i: (i, 0, 0)), vmem()),
        scratch_shapes=[pltpu.VMEM((NR, SEG, DIM), BF16)],
        compiler_params=params(32),
        cost_estimate=pl.CostEstimate(
            flops=2 * 256 * 4096 * 4096, transcendentals=4096 * 4096, bytes_accessed=1 << 25
        ),
        name="affinity",
    )(jnp.stack([z, core]), columns, *pairs, four, across(four))
    degree = to_all(degree, COLS)
    mine, other, own = pl.pallas_call(
        apply_kernel,
        out_shape=(shape(HALF, VEC, SEG), shape(HALF, VEC, SEG), shape(1, SEG)),
        in_specs=[smem(), vmem(), vmem(), pl.BlockSpec(memory_space=pl.ANY)],
        out_specs=(vmem(), vmem(), vmem()),
        scratch_shapes=[
            pltpu.VMEM((NC, SEG), F32),
            pltpu.VMEM((DEPTH, NR * SEG, SEG), BF16),
            pltpu.SemaphoreType.DMA((DEPTH,)),
        ],
        compiler_params=params(44),
        name="apply",
    )(jnp.stack([core, column]), degree, columns, block)
    product = to_all(mine + across(other), "z")
    projected, gram = pl.pallas_call(
        project_kernel,
        out_shape=(shape(VEC, SEG), shape(2, 128)),
        compiler_params=params(8),
        name="project",
    )(product, own)
    gram = jnp.broadcast_to(gram + across(gram), (CHIPS, 2, 128))
    gram = to_all(gram, ("xl", "z", "y", "xh"))
    basis, triangle = pl.pallas_call(
        finish_kernel,
        out_shape=(shape(VEC, SEG), shape(VEC, VEC)),
        compiler_params=params(8),
        name="finish",
    )(gram, projected)
    return basis.T, triangle


def solution(mesh):
    torus = Mesh(mesh.devices.reshape(SIZES), AXES)
    placed = (P(AXES, None), P(AXES, None))
    return jax.shard_map(
        per_device, mesh=torus, in_specs=placed, out_specs=(P(AXES, None), P()), check_vma=False
    )
```

```python
import jax
import jax.numpy as jnp
from jax import lax
from jax.experimental import pallas as pl
from jax.experimental.pallas import tpu as pltpu
from jax.sharding import Mesh
from jax.sharding import PartitionSpec as P

AXES = ("xl", "z", "core", "y", "xh")
SIZES = (2, 8, 2, 4, 2)
ROWS = ("z", "core")
COLS = ("xl", "y", "xh")
CHIPS = 128
HALF = 8
NR = 16
NC = 16
SEG = 256
DIM = 192
VEC = 16
WIDE = DIM + 2 * VEC
SCALE = 14.426950408889634
UNSCALE = 4.5399929762484854e-05
EPS = 1e-6
MIB = 1 << 20
F32 = jnp.float32
BF16 = jnp.bfloat16
HI = lax.Precision.HIGHEST


def params(mib):
    return pltpu.CompilerParams(vmem_limit_bytes=mib * MIB)


def vmem():
    return pl.BlockSpec(memory_space=pltpu.VMEM)


def smem():
    return pl.BlockSpec(memory_space=pltpu.SMEM)


def nt(a, b, **kw):
    return lax.dot_general(a, b, (((1,), (1,)), ((), ())), preferred_element_type=F32, **kw)


def unit_kernel(e_ref, v_ref, u_ref, many_ref):
    e = e_ref[...].astype(F32)
    u = (e * lax.rsqrt(jnp.sum(e * e, axis=0, keepdims=True) + EPS)).astype(BF16)
    u_ref[...] = u
    v = v_ref[...]
    high = v.astype(BF16)
    low = (v - high.astype(F32)).astype(BF16)
    for k in range(NC):
        many_ref[k, 0:DIM, :] = u
        many_ref[k, DIM : DIM + VEC, :] = high
        many_ref[k, DIM + VEC : WIDE, :] = low


def affinity_kernel(pos_ref, t_ref, *refs):
    pairs, lone = refs[0:7], refs[7:9]
    b_ref, deg_ref, s_ref = refs[9:12]
    z, core = pos_ref[2], pos_ref[0]
    step = pl.program_id(0)

    def place(chip, side, rows):
        s_ref[lax.rem(chip + 16, 8) * 2 + side] = rows.T

    @pl.when(step == 0)
    def _():
        sign = 1 - 2 * core
        place(z, core, pairs[0][0])
        place(z, 1 - core, pairs[0][1])
        for k in range(1, 4):
            place(z - k * sign, core, pairs[2 * k - 1][0])
            place(z - k * sign, 1 - core, pairs[2 * k - 1][1])
            place(z + k * sign, 1 - core, pairs[2 * k][0])
            place(z + k * sign, core, pairs[2 * k][1])
        place(z + 4, core, lone[0][...])
        place(z + 4, 1 - core, lone[1][...])

    for j in range(2):
        piece = t_ref[step * 2 + j, 0:DIM, :]
        total = jnp.zeros((8, SEG), F32)
        for r in range(NR):
            score = jnp.dot(s_ref[r], piece, preferred_element_type=F32)
            tile = jnp.exp2(score * SCALE)
            total = total + jnp.sum(tile.reshape(SEG // 8, 8, SEG), axis=0)
            b_ref[step * 2 + j, r * SEG : (r + 1) * SEG, :] = tile.astype(BF16)
        sums = jnp.sum(total, axis=0, keepdims=True) * UNSCALE
        deg_ref[pl.ds(step * 2 + j, 1), :] = sums


def apply_kernel(pos_ref, d0_ref, d1_ref, d2_ref, d3_ref, t_ref, b_ref, mine_ref, other_ref, own_ref, root_ref):
    root_ref[...] = lax.rsqrt((d0_ref[...] + d2_ref[...]) + (d1_ref[...] + d3_ref[...]))
    core = pos_ref[0]
    own_ref[...] = root_ref[pl.ds(pos_ref[1], 1), :] * UNSCALE
    for t in range(NC):
        v = t_ref[t, DIM : DIM + VEC, :].astype(F32) + t_ref[t, DIM + VEC : WIDE, :].astype(F32)
        w = (v * root_ref[t : t + 1, :]).astype(BF16)
        for r in range(NR // 2):
            for side, p_ref in ((core, mine_ref), (1 - core, other_ref)):
                rows = pl.ds(pl.multiple_of((r * 2 + side) * SEG, SEG), SEG)
                part = nt(w, b_ref[t, rows, :])
                p_ref[r] = part if t == 0 else p_ref[r] + part


def project_kernel(p_ref, own_ref, q_ref, gram_ref):
    q = jnp.sum(p_ref[...], axis=0) * own_ref[...]
    q_ref[...] = q
    down = jnp.concatenate([jnp.broadcast_to(q[a : a + 1], (VEC, SEG)) for a in range(VEC)], axis=0)
    pairs = down * jnp.concatenate([q] * VEC, axis=0)
    gram = nt(jnp.ones((8, SEG), F32), pairs, precision=HI)[0:1]
    flat = jnp.concatenate([gram[:, 0:128], gram[:, 128:256]], axis=0)
    gram_ref[...] = flat


def finish_kernel(gram_ref, q_ref, basis_ref, triangle_ref):
    flat = jnp.sum(gram_ref[...], axis=0)
    row = lax.broadcasted_iota(jnp.int32, (VEC, 128), 0)
    lane = lax.broadcasted_iota(jnp.int32, (VEC, 128), 1)
    low = jnp.where(lane // VEC == row, flat[0:1], 0.0)
    high = jnp.where(lane // VEC == row - 8, flat[1:2], 0.0)
    pick = jnp.where(
        lax.broadcasted_iota(jnp.int32, (128, 128), 0) % VEC
        == lax.broadcasted_iota(jnp.int32, (128, 128), 1),
        1.0,
        0.0,
    )
    g = jnp.dot(low + high, pick, preferred_element_type=F32, precision=HI)
    q = q_ref[...]
    wide = lax.broadcasted_iota(jnp.int32, (VEC, SEG), 0)
    for k in range(VEC):
        column = jnp.sum(jnp.where(lane == k, g, 0.0), axis=1, keepdims=True)
        inverse = lax.rsqrt(column[k : k + 1, :])
        factor = column * inverse
        top_g = g[k : k + 1, :] * inverse
        top_q = q[k : k + 1, :] * inverse
        g = jnp.where(row == k, top_g, jnp.where(row > k, g - factor * top_g, g))
        q = jnp.where(wide == k, top_q, jnp.where(wide > k, q - factor * top_q, q))
    basis_ref[...] = q
    triangle_ref[...] = jnp.where(lane >= row, g, 0.0)[:, 0:VEC]


def to_all(copies, axes):
    return lax.all_to_all(copies, axes, split_axis=0, concat_axis=0, tiled=True)


def shape(*dims, dtype=F32):
    return jax.ShapeDtypeStruct(dims, dtype)


def across(a):
    return lax.ppermute(a, "core", [(0, 1), (1, 0)])


def along(a, hops):
    turns = []
    for z in range(8):
        turns += [(z * 2, (z + hops) % 8 * 2), (z * 2 + 1, (z - hops) % 8 * 2 + 1)]
    return lax.ppermute(a, ROWS, turns)


def ring_copies(a, axes, crossed):
    def place(k):
        return k % 4 % 2 * 2 + k % 4 // 2 if crossed else k % 4

    turned = [
        lax.ppermute(a, axes, [(place(k), place(k + hops)) for k in range(4)]) for hops in (1, 2, 3)
    ]
    return [a, *turned]


def per_device(embeddings, vectors):
    z, core = lax.axis_index("z"), lax.axis_index("core")
    position = jnp.stack([core, lax.axis_index(COLS), z])
    unit, unit_copies = pl.pallas_call(
        unit_kernel,
        out_shape=(shape(DIM, SEG, dtype=BF16), shape(NC, WIDE, SEG, dtype=BF16)),
        name="unit",
    )(embeddings.T, vectors.T)
    columns = to_all(unit_copies, COLS)
    pair = jnp.stack([unit, across(unit)])
    one, two = along(pair, 1), along(pair, 2)
    three, four = along(two, 1), along(two[0], 2)
    pairs = (pair, one, across(one), two, across(two), three, across(three))
    block, degree = pl.pallas_call(
        affinity_kernel,
        grid=(NC // 2,),
        out_shape=(pltpu.VMEM((NC, NR * SEG, SEG), BF16), shape(NC, SEG)),
        in_specs=[smem()] + [vmem()] * 10,
        out_specs=(vmem(), vmem()),
        scratch_shapes=[pltpu.VMEM((NR, SEG, DIM), BF16)],
        compiler_params=params(24),
        cost_estimate=pl.CostEstimate(
            flops=2 * 256 * 4096 * 4096, transcendentals=4096 * 4096, bytes_accessed=1 << 25
        ),
        name="affinity",
    )(position, columns, *pairs, four, across(four))
    degree = sum(ring_copies(degree, "y", False))
    degrees = ring_copies(degree, ("xl", "xh"), True)
    mine, other, own = pl.pallas_call(
        apply_kernel,
        out_shape=(shape(HALF, VEC, SEG), shape(HALF, VEC, SEG), shape(1, SEG)),
        in_specs=[smem()] + [vmem()] * 6,
        out_specs=(vmem(), vmem(), vmem()),
        scratch_shapes=[
            pltpu.VMEM((NC, SEG), F32),
        ],
        compiler_params=params(24),
        name="apply",
    )(position, *degrees, columns, pltpu.with_memory_space_constraint(block, pltpu.VMEM))
    product = to_all(mine + across(other), "z")
    projected, gram = pl.pallas_call(
        project_kernel,
        out_shape=(shape(VEC, SEG), shape(2, 128)),
        compiler_params=params(8),
        name="project",
    )(product, own)
    gram = jnp.broadcast_to(gram + across(gram), (CHIPS, 2, 128))
    gram = to_all(gram, ("xl", "z", "y", "xh"))
    basis, triangle = pl.pallas_call(
        finish_kernel,
        out_shape=(shape(VEC, SEG), shape(VEC, VEC)),
        compiler_params=params(8),
        name="finish",
    )(gram, projected)
    return basis.T, triangle


def solution(mesh):
    torus = Mesh(mesh.devices.reshape(SIZES), AXES)
    placed = (P(AXES, None), P(AXES, None))
    return jax.shard_map(
        per_device, mesh=torus, in_specs=placed, out_specs=(P(AXES, None), P()), check_vma=False
    )
```

```python
import jax
import jax.numpy as jnp
from jax import lax
from jax.experimental import pallas as pl
from jax.experimental.pallas import tpu as pltpu
from jax.sharding import Mesh
from jax.sharding import PartitionSpec as P

AXES = ("xl", "z", "core", "y", "xh")
SIZES = (2, 8, 2, 4, 2)
ROWS = ("z", "core")
COLS = ("xl", "y", "xh")
CHIPS = 128
HALF = 8
NR = 16
NC = 16
SEG = 256
DIM = 192
VEC = 16
WIDE = DIM + VEC
SCALE = 14.426950408889634
UNSCALE = 4.5399929762484854e-05
EPS = 1e-6
MIB = 1 << 20
F32 = jnp.float32
BF16 = jnp.bfloat16
HI = lax.Precision.HIGHEST


def params(mib):
    return pltpu.CompilerParams(vmem_limit_bytes=mib * MIB)


def vmem():
    return pl.BlockSpec(memory_space=pltpu.VMEM)


def smem():
    return pl.BlockSpec(memory_space=pltpu.SMEM)


def nt(a, b, **kw):
    return lax.dot_general(a, b, (((1,), (1,)), ((), ())), preferred_element_type=F32, **kw)


def unit_kernel(e_ref, v_ref, u_ref, many_ref):
    e = e_ref[...].astype(F32)
    u = (e * lax.rsqrt(jnp.sum(e * e, axis=0, keepdims=True) + EPS)).astype(BF16)
    u_ref[...] = u
    v = v_ref[...].astype(BF16)
    for k in range(NC):
        many_ref[k, 0:DIM, :] = u
        many_ref[k, DIM:WIDE, :] = v


def affinity_kernel(pos_ref, t_ref, *refs):
    pairs, lone = refs[0:7], refs[7:9]
    b_ref, deg_ref, v_ref, s_ref, c_ref, acc_ref = refs[9:15]
    z, core = pos_ref[2], pos_ref[0]
    step = pl.program_id(0)

    def place(chip, side, rows):
        s_ref[lax.rem(chip + 16, 8) * 2 + side] = rows

    @pl.when(step == 0)
    def _():
        sign = 1 - 2 * core
        place(z, core, pairs[0][0])
        place(z, 1 - core, pairs[0][1])
        for k in range(1, 4):
            place(z - k * sign, core, pairs[2 * k - 1][0])
            place(z - k * sign, 1 - core, pairs[2 * k - 1][1])
            place(z + k * sign, 1 - core, pairs[2 * k][0])
            place(z + k * sign, core, pairs[2 * k][1])
        place(z + 4, core, lone[0][...])
        place(z + 4, 1 - core, lone[1][...])
        for t in range(NC):
            c_ref[t] = t_ref[t, 0:DIM, :].T
            v_ref[t] = t_ref[t, DIM:WIDE, :]
        acc_ref[...] = jnp.zeros_like(acc_ref)

    for t in range(NC):
        total = acc_ref[t]
        for j in range(2):
            score = jnp.dot(c_ref[t], s_ref[step * 2 + j], preferred_element_type=F32)
            tile = jnp.exp2(score * SCALE)
            total = total + (tile[:, 0:128] + tile[:, 128:256])
            b_ref[step * 2 + j, t * SEG : (t + 1) * SEG, :] = tile.astype(BF16)
        acc_ref[t] = total

    @pl.when(step == NR // 2 - 1)
    def _():
        for t in range(NC):
            sums = nt(jnp.ones((8, 128), F32), acc_ref[t], precision=HI)
            deg_ref[t : t + 1, :] = sums[0:1, :] * UNSCALE


def apply_kernel(pos_ref, d0_ref, d1_ref, d2_ref, d3_ref, v_ref, b_ref, *refs):
    mine_ref, other_ref, own_ref, root_ref, w_ref = refs
    core = pos_ref[0]
    root_ref[...] = lax.rsqrt((d0_ref[...] + d2_ref[...]) + (d1_ref[...] + d3_ref[...]))
    own_ref[...] = root_ref[pl.ds(pos_ref[1], 1), :] * UNSCALE
    for t in range(NC):
        w = v_ref[t].astype(F32) * root_ref[t : t + 1, :]
        w_ref[:, t * SEG : (t + 1) * SEG] = w.astype(BF16)
    for r in range(NR // 2):
        for side, p_ref in ((core, mine_ref), (1 - core, other_ref)):
            p_ref[r] = jnp.dot(w_ref[...], b_ref[r * 2 + side], preferred_element_type=F32)


def project_kernel(p_ref, own_ref, q_ref, gram_ref):
    q = jnp.sum(p_ref[...], axis=0) * own_ref[...]
    q_ref[...] = q
    down = jnp.concatenate([jnp.broadcast_to(q[a : a + 1], (VEC, SEG)) for a in range(VEC)], axis=0)
    pairs = down * jnp.concatenate([q] * VEC, axis=0)
    gram = nt(jnp.ones((8, SEG), F32), pairs, precision=HI)[0:1]
    flat = jnp.concatenate([gram[:, 0:128], gram[:, 128:256]], axis=0)
    gram_ref[...] = flat


def finish_kernel(gram_ref, q_ref, basis_ref, triangle_ref):
    flat = jnp.sum(gram_ref[...], axis=0)
    row = lax.broadcasted_iota(jnp.int32, (VEC, 128), 0)
    lane = lax.broadcasted_iota(jnp.int32, (VEC, 128), 1)
    low = jnp.where(lane // VEC == row, flat[0:1], 0.0)
    high = jnp.where(lane // VEC == row - 8, flat[1:2], 0.0)
    pick = jnp.where(
        lax.broadcasted_iota(jnp.int32, (128, 128), 0) % VEC
        == lax.broadcasted_iota(jnp.int32, (128, 128), 1),
        1.0,
        0.0,
    )
    g = jnp.dot(low + high, pick, preferred_element_type=F32, precision=HI)
    q = q_ref[...]
    wide = lax.broadcasted_iota(jnp.int32, (VEC, SEG), 0)
    for k in range(VEC):
        column = jnp.sum(jnp.where(lane == k, g, 0.0), axis=1, keepdims=True)
        inverse = lax.rsqrt(column[k : k + 1, :])
        factor = column * inverse
        top_g = g[k : k + 1, :] * inverse
        top_q = q[k : k + 1, :] * inverse
        g = jnp.where(row == k, top_g, jnp.where(row > k, g - factor * top_g, g))
        q = jnp.where(wide == k, top_q, jnp.where(wide > k, q - factor * top_q, q))
    basis_ref[...] = q
    triangle_ref[...] = jnp.where(lane >= row, g, 0.0)[:, 0:VEC]


def to_all(copies, axes):
    return lax.all_to_all(copies, axes, split_axis=0, concat_axis=0, tiled=True)


def shape(*dims, dtype=F32):
    return jax.ShapeDtypeStruct(dims, dtype)


def across(a):
    return lax.ppermute(a, "core", [(0, 1), (1, 0)])


def along(a, hops):
    turns = []
    for z in range(8):
        turns += [(z * 2, (z + hops) % 8 * 2), (z * 2 + 1, (z - hops) % 8 * 2 + 1)]
    return lax.ppermute(a, ROWS, turns)


def ring_copies(a, axes, crossed):
    def place(k):
        return k % 4 % 2 * 2 + k % 4 // 2 if crossed else k % 4

    turned = [
        lax.ppermute(a, axes, [(place(k), place(k + hops)) for k in range(4)]) for hops in (1, 2, 3)
    ]
    return [a, *turned]


def per_device(embeddings, vectors):
    z, core = lax.axis_index("z"), lax.axis_index("core")
    position = jnp.stack([core, lax.axis_index(COLS), z])
    unit, unit_copies = pl.pallas_call(
        unit_kernel,
        out_shape=(shape(DIM, SEG, dtype=BF16), shape(NC, WIDE, SEG, dtype=BF16)),
        name="unit",
    )(embeddings.T, vectors.T)
    columns = pltpu.with_memory_space_constraint(to_all(unit_copies, COLS), pltpu.HBM)
    pair = jnp.stack([unit, across(unit)])
    one, two = along(pair, 1), along(pair, 2)
    three, four = along(two, 1), along(two[0], 2)
    pairs = (pair, one, across(one), two, across(two), three, across(three))
    block, degree, vector_columns = pl.pallas_call(
        affinity_kernel,
        grid=(NC // 2,),
        out_shape=(
            pltpu.VMEM((NR, NC * SEG, SEG), BF16),
            shape(NC, SEG),
            shape(NC, VEC, SEG, dtype=BF16),
        ),
        in_specs=[smem()] + [vmem()] * 10,
        out_specs=(vmem(), vmem(), vmem()),
        scratch_shapes=[
            pltpu.VMEM((NR, DIM, SEG), BF16),
            pltpu.VMEM((NC, SEG, DIM), BF16),
            pltpu.VMEM((NC, SEG, 128), F32),
        ],
        compiler_params=params(24),
        cost_estimate=pl.CostEstimate(
            flops=2 * 256 * 4096 * 4096, transcendentals=4096 * 4096, bytes_accessed=1 << 25
        ),
        name="affinity",
    )(position, columns, *pairs, four, across(four))
    degree = sum(ring_copies(degree, "y", False))
    degrees = ring_copies(degree, ("xl", "xh"), True)
    mine, other, own = pl.pallas_call(
        apply_kernel,
        out_shape=(shape(HALF, VEC, SEG), shape(HALF, VEC, SEG), shape(1, SEG)),
        in_specs=[smem()] + [vmem()] * 6,
        out_specs=(vmem(), vmem(), vmem()),
        scratch_shapes=[
            pltpu.VMEM((NC, SEG), F32),
            pltpu.VMEM((VEC, NC * SEG), BF16),
        ],
        compiler_params=params(24),
        name="apply",
    )(position, *degrees, vector_columns, pltpu.with_memory_space_constraint(block, pltpu.VMEM))
    product = to_all(mine + across(other), "z")
    projected, gram = pl.pallas_call(
        project_kernel,
        out_shape=(shape(VEC, SEG), shape(2, 128)),
        compiler_params=params(8),
        name="project",
    )(product, own)
    gram = jnp.broadcast_to(gram + across(gram), (CHIPS, 2, 128))
    gram = to_all(gram, ("xl", "z", "y", "xh"))
    basis, triangle = pl.pallas_call(
        finish_kernel,
        out_shape=(shape(VEC, SEG), shape(VEC, VEC)),
        compiler_params=params(8),
        name="finish",
    )(gram, projected)
    return basis.T, triangle


def solution(mesh):
    torus = Mesh(mesh.devices.reshape(SIZES), AXES)
    placed = (P(AXES, None), P(AXES, None))
    return jax.shard_map(
        per_device, mesh=torus, in_specs=placed, out_specs=(P(AXES, None), P()), check_vma=False
    )
```

```python
import jax
import jax.numpy as jnp
from jax import lax
from jax.experimental import pallas as pl
from jax.experimental.pallas import tpu as pltpu
from jax.sharding import Mesh
from jax.sharding import PartitionSpec as P

AXES = ("xl", "zh", "zl", "core", "y", "xh")
SIZES = (2, 4, 2, 2, 4, 2)
ROWS = ("zh", "zl", "core")
COLS = ("xl", "y", "xh")
CHIPS = 128
QUARTER = 4
NR = 16
NC = 16
SEG = 256
DIM = 192
VEC = 16
WIDE = DIM + 2 * VEC
SCALE = 14.426950408889634
UNSCALE = 4.5399929762484854e-05
EPS = 1e-6
MIB = 1 << 20
F32 = jnp.float32
BF16 = jnp.bfloat16
HI = lax.Precision.HIGHEST


def params(mib):
    return pltpu.CompilerParams(vmem_limit_bytes=mib * MIB)


def vmem():
    return pl.BlockSpec(memory_space=pltpu.VMEM)


def smem():
    return pl.BlockSpec(memory_space=pltpu.SMEM)


def nt(a, b, **kw):
    return lax.dot_general(a, b, (((1,), (1,)), ((), ())), preferred_element_type=F32, **kw)


def unit_kernel(e_ref, v_ref, u_ref, many_ref):
    e = e_ref[...].astype(F32)
    u = (e * lax.rsqrt(jnp.sum(e * e, axis=0, keepdims=True) + EPS)).astype(BF16)
    u_ref[...] = u
    v = v_ref[...]
    high = v.astype(BF16)
    low = (v - high.astype(F32)).astype(BF16)
    for k in range(NC):
        many_ref[k, 0:DIM, :] = u
        many_ref[k, DIM : DIM + VEC, :] = high
        many_ref[k, DIM + VEC : WIDE, :] = low


def affinity_kernel(pos_ref, t_ref, *refs):
    pairs, lone = refs[0:7], refs[7:9]
    b_ref, deg_ref, v_ref, s_ref, c_ref, acc_ref = refs[9:15]
    z, core = pos_ref[2], pos_ref[0]
    step = pl.program_id(0)

    def place(chip, side, rows):
        s_ref[lax.rem(chip + 16, 8) * 2 + side] = rows

    @pl.when(step == 0)
    def _():
        sign = 1 - 2 * core
        place(z, core, pairs[0][0])
        place(z, 1 - core, pairs[0][1])
        for k in range(1, 4):
            place(z - k * sign, core, pairs[2 * k - 1][0])
            place(z - k * sign, 1 - core, pairs[2 * k - 1][1])
            place(z + k * sign, 1 - core, pairs[2 * k][0])
            place(z + k * sign, core, pairs[2 * k][1])
        place(z + 4, core, lone[0][...])
        place(z + 4, 1 - core, lone[1][...])
        for t in range(NC):
            c_ref[t] = t_ref[t, 0:DIM, :].T
            high = t_ref[t, DIM : DIM + VEC, :].astype(F32)
            v_ref[t] = high + t_ref[t, DIM + VEC : WIDE, :].astype(F32)
        acc_ref[...] = jnp.zeros_like(acc_ref)

    for t in range(NC):
        total = acc_ref[t]
        for j in range(2):
            score = jnp.dot(c_ref[t], s_ref[step * 2 + j], preferred_element_type=F32)
            tile = jnp.exp2(score * SCALE)
            total = total + (tile[:, 0:128] + tile[:, 128:256])
            b_ref[step * 2 + j, t * SEG : (t + 1) * SEG, :] = tile.astype(BF16)
        acc_ref[t] = total

    @pl.when(step == NR // 2 - 1)
    def _():
        for t in range(NC):
            sums = nt(jnp.ones((8, 128), F32), acc_ref[t], precision=HI)
            deg_ref[t : t + 1, :] = sums[0:1, :] * UNSCALE


def apply_kernel(pos_ref, d0_ref, d1_ref, d2_ref, d3_ref, v_ref, b_ref, *refs):
    p_refs, (own_ref, root_ref, w_ref) = refs[0:4], refs[4:7]
    core, low = pos_ref[0], lax.rem(pos_ref[2], 2)
    root_ref[...] = lax.rsqrt((d0_ref[...] + d2_ref[...]) + (d1_ref[...] + d3_ref[...]))
    own_ref[...] = root_ref[pl.ds(pos_ref[1], 1), :] * UNSCALE
    for t in range(NC):
        w = v_ref[t] * root_ref[t : t + 1, :]
        w_ref[:, t * SEG : (t + 1) * SEG] = w.astype(BF16)
    for k, p_ref in enumerate(p_refs):
        side = core if k % 2 == 0 else 1 - core
        chip = low if k < 2 else 1 - low
        for high in range(QUARTER):
            rows = b_ref[high * 4 + chip * 2 + side]
            p_ref[high] = jnp.dot(w_ref[...], rows, preferred_element_type=F32)


def project_kernel(p_ref, own_ref, q_ref, gram_ref):
    q = jnp.sum(p_ref[...], axis=0) * own_ref[...]
    q_ref[...] = q
    down = jnp.concatenate([jnp.broadcast_to(q[a : a + 1], (VEC, SEG)) for a in range(VEC)], axis=0)
    pairs = down * jnp.concatenate([q] * VEC, axis=0)
    gram = nt(jnp.ones((8, SEG), F32), pairs, precision=HI)[0:1]
    flat = jnp.concatenate([gram[:, 0:128], gram[:, 128:256]], axis=0)
    gram_ref[...] = flat


def finish_kernel(gram_ref, q_ref, basis_ref, triangle_ref):
    flat = jnp.sum(gram_ref[...], axis=0)
    row = lax.broadcasted_iota(jnp.int32, (VEC, 128), 0)
    lane = lax.broadcasted_iota(jnp.int32, (VEC, 128), 1)
    low = jnp.where(lane // VEC == row, flat[0:1], 0.0)
    high = jnp.where(lane // VEC == row - 8, flat[1:2], 0.0)
    pick = jnp.where(
        lax.broadcasted_iota(jnp.int32, (128, 128), 0) % VEC
        == lax.broadcasted_iota(jnp.int32, (128, 128), 1),
        1.0,
        0.0,
    )
    g = jnp.dot(low + high, pick, preferred_element_type=F32, precision=HI)
    q = q_ref[...]
    wide = lax.broadcasted_iota(jnp.int32, (VEC, SEG), 0)
    for k in range(VEC):
        column = jnp.sum(jnp.where(lane == k, g, 0.0), axis=1, keepdims=True)
        inverse = lax.rsqrt(column[k : k + 1, :])
        factor = column * inverse
        top_g = g[k : k + 1, :] * inverse
        top_q = q[k : k + 1, :] * inverse
        g = jnp.where(row == k, top_g, jnp.where(row > k, g - factor * top_g, g))
        q = jnp.where(wide == k, top_q, jnp.where(wide > k, q - factor * top_q, q))
    basis_ref[...] = q
    triangle_ref[...] = jnp.where(lane >= row, g, 0.0)[:, 0:VEC]


def to_all(copies, axes):
    return lax.all_to_all(copies, axes, split_axis=0, concat_axis=0, tiled=True)


def shape(*dims, dtype=F32):
    return jax.ShapeDtypeStruct(dims, dtype)


def across(a):
    return lax.ppermute(a, "core", [(0, 1), (1, 0)])


def along(a, hops):
    turns = []
    for z in range(8):
        turns += [(z * 2, (z + hops) % 8 * 2), (z * 2 + 1, (z - hops) % 8 * 2 + 1)]
    return lax.ppermute(a, ROWS, turns)


def ring_copies(a, axes, crossed):
    def place(k):
        return k % 4 % 2 * 2 + k % 4 // 2 if crossed else k % 4

    turned = [
        lax.ppermute(a, axes, [(place(k), place(k + hops)) for k in range(4)]) for hops in (1, 2, 3)
    ]
    return [a, *turned]


def per_device(embeddings, vectors):
    z, core = lax.axis_index(("zh", "zl")), lax.axis_index("core")
    position = jnp.stack([core, lax.axis_index(COLS), z])
    unit, unit_copies = pl.pallas_call(
        unit_kernel,
        out_shape=(shape(DIM, SEG, dtype=BF16), shape(NC, WIDE, SEG, dtype=BF16)),
        name="unit",
    )(embeddings.T, vectors.T)
    columns = pltpu.with_memory_space_constraint(to_all(unit_copies, COLS), pltpu.HBM)
    pair = jnp.stack([unit, across(unit)])
    one, two = along(pair, 1), along(pair, 2)
    three, four = along(two, 1), along(two[0], 2)
    pairs = (pair, one, across(one), two, across(two), three, across(three))
    block, degree, vector_columns = pl.pallas_call(
        affinity_kernel,
        grid=(NC // 2,),
        out_shape=(
            pltpu.VMEM((NR, NC * SEG, SEG), BF16),
            shape(NC, SEG),
            shape(NC, VEC, SEG),
        ),
        in_specs=[smem()] + [vmem()] * 10,
        out_specs=(vmem(), vmem(), vmem()),
        scratch_shapes=[
            pltpu.VMEM((NR, DIM, SEG), BF16),
            pltpu.VMEM((NC, SEG, DIM), BF16),
            pltpu.VMEM((NC, SEG, 128), F32),
        ],
        compiler_params=params(24),
        cost_estimate=pl.CostEstimate(
            flops=2 * 256 * 4096 * 4096, transcendentals=4096 * 4096, bytes_accessed=1 << 25
        ),
        name="affinity",
    )(position, columns, *pairs, four, across(four))
    degree = sum(ring_copies(degree, "y", False))
    degrees = ring_copies(degree, ("xl", "xh"), True)
    *parts, own = pl.pallas_call(
        apply_kernel,
        out_shape=(*[shape(QUARTER, VEC, SEG)] * 4, shape(1, SEG)),
        in_specs=[smem()] + [vmem()] * 6,
        out_specs=(vmem(),) * 5,
        scratch_shapes=[
            pltpu.VMEM((NC, SEG), F32),
            pltpu.VMEM((VEC, NC * SEG), BF16),
        ],
        compiler_params=params(24),
        name="apply",
    )(position, *degrees, vector_columns, pltpu.with_memory_space_constraint(block, pltpu.VMEM))
    beside = lax.ppermute(parts[2], "zl", [(0, 1), (1, 0)])
    corner = lax.ppermute(parts[3], ("zl", "core"), [(k, 3 - k) for k in range(4)])
    product = (parts[0] + across(parts[1])) + (beside + corner)
    product = to_all(product, "zh")
    projected, gram = pl.pallas_call(
        project_kernel,
        out_shape=(shape(VEC, SEG), shape(2, 128)),
        compiler_params=params(8),
        name="project",
    )(product, own)
    gram = jnp.broadcast_to(gram + across(gram), (CHIPS, 2, 128))
    gram = to_all(gram, ("xl", "zh", "zl", "y", "xh"))
    basis, triangle = pl.pallas_call(
        finish_kernel,
        out_shape=(shape(VEC, SEG), shape(VEC, VEC)),
        compiler_params=params(8),
        name="finish",
    )(gram, projected)
    return basis.T, triangle


def solution(mesh):
    torus = Mesh(mesh.devices.reshape(SIZES), AXES)
    placed = (P(AXES, None), P(AXES, None))
    return jax.shard_map(
        per_device, mesh=torus, in_specs=placed, out_specs=(P(AXES, None), P()), check_vma=False
    )
```

```python
import jax
import jax.numpy as jnp
from jax import lax
from jax.experimental import pallas as pl
from jax.experimental.pallas import tpu as pltpu
from jax.sharding import Mesh
from jax.sharding import PartitionSpec as P

AXES = ("xl", "z", "core", "y", "xh")
SIZES = (2, 8, 2, 4, 2)
ROWS = ("z", "core")
COLS = ("xl", "y", "xh")
CHIPS = 128
HALF = 8
NR = 16
NC = 16
SEG = 256
DIM = 192
VEC = 16
WIDE = DIM + VEC
DEPTH = 6
SCALE = 14.426950408889634
UNSCALE = 4.5399929762484854e-05
EPS = 1e-6
MIB = 1 << 20
F32 = jnp.float32
BF16 = jnp.bfloat16
HI = lax.Precision.HIGHEST


def params(mib):
    return pltpu.CompilerParams(vmem_limit_bytes=mib * MIB)


def vmem():
    return pl.BlockSpec(memory_space=pltpu.VMEM)


def smem():
    return pl.BlockSpec(memory_space=pltpu.SMEM)


def nt(a, b, **kw):
    return lax.dot_general(a, b, (((1,), (1,)), ((), ())), preferred_element_type=F32, **kw)


def unit_kernel(e_ref, v_ref, u_ref, many_ref):
    e = e_ref[...].astype(F32)
    u = (e * lax.rsqrt(jnp.sum(e * e, axis=0, keepdims=True) + EPS)).astype(BF16)
    u_ref[...] = u
    v = v_ref[...].astype(BF16)
    for k in range(NC):
        many_ref[k, 0:DIM, :] = u
        many_ref[k, DIM:WIDE, :] = v


def affinity_kernel(pos_ref, t_ref, *refs):
    pairs, lone = refs[0:7], refs[7:9]
    b_ref, deg_ref, s_ref = refs[9:12]
    z, core = pos_ref[0], pos_ref[1]
    step = pl.program_id(0)

    def place(chip, side, rows):
        s_ref[lax.rem(chip + 16, 8) * 2 + side] = rows.T

    @pl.when(step == 0)
    def _():
        sign = 1 - 2 * core
        place(z, core, pairs[0][0])
        place(z, 1 - core, pairs[0][1])
        for k in range(1, 4):
            place(z - k * sign, core, pairs[2 * k - 1][0])
            place(z - k * sign, 1 - core, pairs[2 * k - 1][1])
            place(z + k * sign, 1 - core, pairs[2 * k][0])
            place(z + k * sign, core, pairs[2 * k][1])
        place(z + 4, core, lone[0][...])
        place(z + 4, 1 - core, lone[1][...])

    for j in range(2):
        piece = t_ref[step * 2 + j, 0:DIM, :]
        total = jnp.zeros((8, SEG), F32)
        for r in range(NR):
            score = jnp.dot(s_ref[r], piece, preferred_element_type=F32)
            tile = jnp.exp2(score * SCALE)
            total = total + jnp.sum(tile.reshape(SEG // 8, 8, SEG), axis=0)
            b_ref[j, r * SEG : (r + 1) * SEG, :] = tile.astype(BF16)
        sums = jnp.sum(total, axis=0, keepdims=True) * UNSCALE
        for k in range(NC):
            deg_ref[k, pl.ds(step * 2 + j, 1), :] = sums


def apply_kernel(pos_ref, deg_ref, t_ref, b_ref, mine_ref, other_ref, own_ref, root_ref, held_ref, sem_ref):
    def fetch(t):
        slot = t % DEPTH
        return pltpu.make_async_copy(b_ref.at[t], held_ref.at[slot], sem_ref.at[slot])

    for t in range(DEPTH):
        fetch(t).start()
    root_ref[...] = lax.rsqrt(jnp.sum(deg_ref[...], axis=0))
    core = pos_ref[0]
    own_ref[...] = root_ref[pl.ds(pos_ref[1], 1), :] * UNSCALE
    for t in range(NC):
        v = t_ref[t, DIM:WIDE, :].astype(F32)
        w = (v * root_ref[t : t + 1, :]).astype(BF16)
        fetch(t).wait()
        for r in range(NR // 2):
            for side, p_ref in ((core, mine_ref), (1 - core, other_ref)):
                rows = pl.ds(pl.multiple_of((r * 2 + side) * SEG, SEG), SEG)
                part = nt(w, held_ref[t % DEPTH, rows, :])
                p_ref[r] = part if t == 0 else p_ref[r] + part
        if t + DEPTH < NC:
            fetch(t + DEPTH).start()


def project_kernel(p_ref, own_ref, q_ref, gram_ref):
    q = jnp.sum(p_ref[...], axis=0) * own_ref[...]
    q_ref[...] = q
    down = jnp.concatenate([jnp.broadcast_to(q[a : a + 1], (VEC, SEG)) for a in range(VEC)], axis=0)
    pairs = down * jnp.concatenate([q] * VEC, axis=0)
    gram = nt(jnp.ones((8, SEG), F32), pairs, precision=HI)[0:1]
    flat = jnp.concatenate([gram[:, 0:128], gram[:, 128:256]], axis=0)
    gram_ref[...] = flat


def finish_kernel(gram_ref, q_ref, basis_ref, triangle_ref):
    flat = jnp.sum(gram_ref[...], axis=0)
    row = lax.broadcasted_iota(jnp.int32, (VEC, 128), 0)
    lane = lax.broadcasted_iota(jnp.int32, (VEC, 128), 1)
    low = jnp.where(lane // VEC == row, flat[0:1], 0.0)
    high = jnp.where(lane // VEC == row - 8, flat[1:2], 0.0)
    pick = jnp.where(
        lax.broadcasted_iota(jnp.int32, (128, 128), 0) % VEC
        == lax.broadcasted_iota(jnp.int32, (128, 128), 1),
        1.0,
        0.0,
    )
    g = jnp.dot(low + high, pick, preferred_element_type=F32, precision=HI)
    q = q_ref[...]
    wide = lax.broadcasted_iota(jnp.int32, (VEC, SEG), 0)
    for k in range(VEC):
        column = jnp.sum(jnp.where(lane == k, g, 0.0), axis=1, keepdims=True)
        inverse = lax.rsqrt(column[k : k + 1, :])
        factor = column * inverse
        top_g = g[k : k + 1, :] * inverse
        top_q = q[k : k + 1, :] * inverse
        g = jnp.where(row == k, top_g, jnp.where(row > k, g - factor * top_g, g))
        q = jnp.where(wide == k, top_q, jnp.where(wide > k, q - factor * top_q, q))
    basis_ref[...] = q
    triangle_ref[...] = jnp.where(lane >= row, g, 0.0)[:, 0:VEC]


def to_all(copies, axes):
    return lax.all_to_all(copies, axes, split_axis=0, concat_axis=0, tiled=True)


def shape(*dims, dtype=F32):
    return jax.ShapeDtypeStruct(dims, dtype)


def across(a):
    return lax.ppermute(a, "core", [(0, 1), (1, 0)])


def along(a, hops):
    turns = []
    for z in range(8):
        turns += [(z * 2, (z + hops) % 8 * 2), (z * 2 + 1, (z - hops) % 8 * 2 + 1)]
    return lax.ppermute(a, ROWS, turns)


def per_device(embeddings, vectors):
    z, core = lax.axis_index("z"), lax.axis_index("core")
    column = lax.axis_index(COLS)
    unit, unit_copies = pl.pallas_call(
        unit_kernel,
        out_shape=(shape(DIM, SEG, dtype=BF16), shape(NC, WIDE, SEG, dtype=BF16)),
        name="unit",
    )(embeddings.T, vectors.T)
    columns = to_all(unit_copies, COLS)
    pair = jnp.stack([unit, across(unit)])
    one, two = along(pair, 1), along(pair, 2)
    three, four = along(two, 1), along(two[0], 2)
    pairs = (pair, one, across(one), two, across(two), three, across(three))
    block, degree = pl.pallas_call(
        affinity_kernel,
        grid=(NC // 2,),
        out_shape=(shape(NC, NR * SEG, SEG, dtype=BF16), shape(NC, NC, SEG)),
        in_specs=[smem()] + [vmem()] * 10,
        out_specs=(pl.BlockSpec((2, NR * SEG, SEG), lambda i: (i, 0, 0)), vmem()),
        scratch_shapes=[pltpu.VMEM((NR, SEG, DIM), BF16)],
        compiler_params=params(32),
        cost_estimate=pl.CostEstimate(
            flops=2 * 256 * 4096 * 4096, transcendentals=4096 * 4096, bytes_accessed=1 << 25
        ),
        name="affinity",
    )(jnp.stack([z, core]), columns, *pairs, four, across(four))
    degree = to_all(degree, COLS)
    mine, other, own = pl.pallas_call(
        apply_kernel,
        out_shape=(shape(HALF, VEC, SEG), shape(HALF, VEC, SEG), shape(1, SEG)),
        in_specs=[smem(), vmem(), vmem(), pl.BlockSpec(memory_space=pl.ANY)],
        out_specs=(vmem(), vmem(), vmem()),
        scratch_shapes=[
            pltpu.VMEM((NC, SEG), F32),
            pltpu.VMEM((DEPTH, NR * SEG, SEG), BF16),
            pltpu.SemaphoreType.DMA((DEPTH,)),
        ],
        compiler_params=params(44),
        name="apply",
    )(jnp.stack([core, column]), degree, columns, block)
    product = to_all(mine + across(other), "z")
    projected, gram = pl.pallas_call(
        project_kernel,
        out_shape=(shape(VEC, SEG), shape(2, 128)),
        compiler_params=params(8),
        name="project",
    )(product, own)
    gram = jnp.broadcast_to(gram + across(gram), (CHIPS, 2, 128))
    gram = to_all(gram, ("xl", "z", "y", "xh"))
    basis, triangle = pl.pallas_call(
        finish_kernel,
        out_shape=(shape(VEC, SEG), shape(VEC, VEC)),
        compiler_params=params(8),
        name="finish",
    )(gram, projected)
    return basis.T, triangle


def solution(mesh):
    torus = Mesh(mesh.devices.reshape(SIZES), AXES)
    placed = (P(AXES, None), P(AXES, None))
    return jax.shard_map(
        per_device, mesh=torus, in_specs=placed, out_specs=(P(AXES, None), P()), check_vma=False
    )
```

```python
import jax
import jax.numpy as jnp
from jax import lax
from jax.experimental import pallas as pl
from jax.experimental.pallas import tpu as pltpu
from jax.sharding import Mesh
from jax.sharding import PartitionSpec as P

AXES = ("xl", "z", "core", "y", "xh")
SIZES = (2, 8, 2, 4, 2)
ROWS = ("z", "core")
COLS = ("xl", "y", "xh")
CHIPS = 128
HALF = 8
NR = 16
NC = 16
SEG = 256
DIM = 192
VEC = 16
WIDE = DIM + VEC
DEPTH = 6
SCALE = 14.426950408889634
UNSCALE = 4.5399929762484854e-05
EPS = 1e-6
MIB = 1 << 20
F32 = jnp.float32
BF16 = jnp.bfloat16
HI = lax.Precision.HIGHEST


def params(mib):
    return pltpu.CompilerParams(vmem_limit_bytes=mib * MIB)


def vmem():
    return pl.BlockSpec(memory_space=pltpu.VMEM)


def smem():
    return pl.BlockSpec(memory_space=pltpu.SMEM)


def nt(a, b, **kw):
    return lax.dot_general(a, b, (((1,), (1,)), ((), ())), preferred_element_type=F32, **kw)


def unit_kernel(e_ref, v_ref, u_ref, many_ref):
    e = e_ref[...].astype(F32)
    u = (e * lax.rsqrt(jnp.sum(e * e, axis=0, keepdims=True) + EPS)).astype(BF16)
    u_ref[...] = u
    v = v_ref[...].astype(BF16)
    for k in range(NC):
        many_ref[k, 0:DIM, :] = u
        many_ref[k, DIM:WIDE, :] = v


def affinity_kernel(pos_ref, t_ref, *refs):
    pairs, lone = refs[0:7], refs[7:9]
    b_ref, deg_ref, s_ref, sum_ref = refs[9:13]
    z, core = pos_ref[0], pos_ref[1]
    step = pl.program_id(0)

    def place(chip, side, rows):
        s_ref[lax.rem(chip + 16, 8) * 2 + side] = rows.T

    @pl.when(step == 0)
    def _():
        sign = 1 - 2 * core
        place(z, core, pairs[0][0])
        place(z, 1 - core, pairs[0][1])
        for k in range(1, 4):
            place(z - k * sign, core, pairs[2 * k - 1][0])
            place(z - k * sign, 1 - core, pairs[2 * k - 1][1])
            place(z + k * sign, 1 - core, pairs[2 * k][0])
            place(z + k * sign, core, pairs[2 * k][1])
        place(z + 4, core, lone[0][...])
        place(z + 4, 1 - core, lone[1][...])

    for j in range(2):
        piece = t_ref[step * 2 + j, 0:DIM, :]
        total = jnp.zeros((8, SEG), F32)
        for r in range(NR):
            score = jnp.dot(s_ref[r], piece, preferred_element_type=F32)
            tile = jnp.exp2(score * SCALE)
            total = total + jnp.sum(tile.reshape(SEG // 8, 8, SEG), axis=0)
            b_ref[j, r * SEG : (r + 1) * SEG, :] = tile.astype(BF16)
        sums = jnp.sum(total, axis=0, keepdims=True) * UNSCALE
        sum_ref[pl.ds(step * 2 + j, 1), :] = sums

    @pl.when(step == NC // 2 - 1)
    def _():
        for k in range(NC):
            deg_ref[k] = sum_ref[...].astype(BF16)


def apply_kernel(pos_ref, deg_ref, t_ref, b_ref, mine_ref, other_ref, own_ref, root_ref, held_ref, sem_ref):
    def fetch(t):
        slot = t % DEPTH
        return pltpu.make_async_copy(b_ref.at[t], held_ref.at[slot], sem_ref.at[slot])

    for t in range(DEPTH):
        fetch(t).start()
    root_ref[...] = lax.rsqrt(jnp.sum(deg_ref[...].astype(F32), axis=0))
    core = pos_ref[0]
    own_ref[...] = root_ref[pl.ds(pos_ref[1], 1), :] * UNSCALE
    for t in range(NC):
        v = t_ref[t, DIM:WIDE, :].astype(F32)
        w = (v * root_ref[t : t + 1, :]).astype(BF16)
        fetch(t).wait()
        for r in range(NR // 2):
            for side, p_ref in ((core, mine_ref), (1 - core, other_ref)):
                rows = pl.ds(pl.multiple_of((r * 2 + side) * SEG, SEG), SEG)
                part = nt(w, held_ref[t % DEPTH, rows, :])
                p_ref[r] = part if t == 0 else p_ref[r] + part
        if t + DEPTH < NC:
            fetch(t + DEPTH).start()


def project_kernel(p_ref, own_ref, q_ref, gram_ref):
    q = jnp.sum(p_ref[...], axis=0) * own_ref[...]
    q_ref[...] = q
    down = jnp.concatenate([jnp.broadcast_to(q[a : a + 1], (VEC, SEG)) for a in range(VEC)], axis=0)
    pairs = down * jnp.concatenate([q] * VEC, axis=0)
    gram = nt(jnp.ones((8, SEG), F32), pairs, precision=HI)[0:1]
    flat = jnp.concatenate([gram[:, 0:128], gram[:, 128:256]], axis=0)
    gram_ref[...] = flat


def finish_kernel(gram_ref, q_ref, basis_ref, triangle_ref):
    flat = jnp.sum(gram_ref[...], axis=0)
    row = lax.broadcasted_iota(jnp.int32, (VEC, 128), 0)
    lane = lax.broadcasted_iota(jnp.int32, (VEC, 128), 1)
    low = jnp.where(lane // VEC == row, flat[0:1], 0.0)
    high = jnp.where(lane // VEC == row - 8, flat[1:2], 0.0)
    pick = jnp.where(
        lax.broadcasted_iota(jnp.int32, (128, 128), 0) % VEC
        == lax.broadcasted_iota(jnp.int32, (128, 128), 1),
        1.0,
        0.0,
    )
    g = jnp.dot(low + high, pick, preferred_element_type=F32, precision=HI)
    q = q_ref[...]
    wide = lax.broadcasted_iota(jnp.int32, (VEC, SEG), 0)
    for k in range(VEC):
        column = jnp.sum(jnp.where(lane == k, g, 0.0), axis=1, keepdims=True)
        inverse = lax.rsqrt(column[k : k + 1, :])
        factor = column * inverse
        top_g = g[k : k + 1, :] * inverse
        top_q = q[k : k + 1, :] * inverse
        g = jnp.where(row == k, top_g, jnp.where(row > k, g - factor * top_g, g))
        q = jnp.where(wide == k, top_q, jnp.where(wide > k, q - factor * top_q, q))
    basis_ref[...] = q
    triangle_ref[...] = jnp.where(lane >= row, g, 0.0)[:, 0:VEC]


def to_all(copies, axes):
    return lax.all_to_all(copies, axes, split_axis=0, concat_axis=0, tiled=True)


def shape(*dims, dtype=F32):
    return jax.ShapeDtypeStruct(dims, dtype)


def across(a):
    return lax.ppermute(a, "core", [(0, 1), (1, 0)])


def along(a, hops):
    turns = []
    for z in range(8):
        turns += [(z * 2, (z + hops) % 8 * 2), (z * 2 + 1, (z - hops) % 8 * 2 + 1)]
    return lax.ppermute(a, ROWS, turns)


def per_device(embeddings, vectors):
    z, core = lax.axis_index("z"), lax.axis_index("core")
    column = lax.axis_index(COLS)
    unit, unit_copies = pl.pallas_call(
        unit_kernel,
        out_shape=(shape(DIM, SEG, dtype=BF16), shape(NC, WIDE, SEG, dtype=BF16)),
        name="unit",
    )(embeddings.T, vectors.T)
    columns = to_all(unit_copies, COLS)
    pair = jnp.stack([unit, across(unit)])
    one, two = along(pair, 1), along(pair, 2)
    three, four = along(two, 1), along(two[0], 2)
    pairs = (pair, one, across(one), two, across(two), three, across(three))
    block, degree = pl.pallas_call(
        affinity_kernel,
        grid=(NC // 2,),
        out_shape=(shape(NC, NR * SEG, SEG, dtype=BF16), shape(NC, NC, SEG, dtype=BF16)),
        in_specs=[smem()] + [vmem()] * 10,
        out_specs=(pl.BlockSpec((2, NR * SEG, SEG), lambda i: (i, 0, 0)), vmem()),
        scratch_shapes=[pltpu.VMEM((NR, SEG, DIM), BF16), pltpu.VMEM((NC, SEG), F32)],
        compiler_params=params(32),
        cost_estimate=pl.CostEstimate(
            flops=2 * 256 * 4096 * 4096, transcendentals=4096 * 4096, bytes_accessed=1 << 25
        ),
        name="affinity",
    )(jnp.stack([z, core]), columns, *pairs, four, across(four))
    degree = to_all(degree, COLS)
    mine, other, own = pl.pallas_call(
        apply_kernel,
        out_shape=(shape(HALF, VEC, SEG), shape(HALF, VEC, SEG), shape(1, SEG)),
        in_specs=[smem(), vmem(), vmem(), pl.BlockSpec(memory_space=pl.ANY)],
        out_specs=(vmem(), vmem(), vmem()),
        scratch_shapes=[
            pltpu.VMEM((NC, SEG), F32),
            pltpu.VMEM((DEPTH, NR * SEG, SEG), BF16),
            pltpu.SemaphoreType.DMA((DEPTH,)),
        ],
        compiler_params=params(44),
        name="apply",
    )(jnp.stack([core, column]), degree, columns, block)
    product = to_all(mine + across(other), "z")
    projected, gram = pl.pallas_call(
        project_kernel,
        out_shape=(shape(VEC, SEG), shape(2, 128)),
        compiler_params=params(8),
        name="project",
    )(product, own)
    gram = jnp.broadcast_to(gram + across(gram), (CHIPS, 2, 128))
    gram = to_all(gram, ("xl", "z", "y", "xh"))
    basis, triangle = pl.pallas_call(
        finish_kernel,
        out_shape=(shape(VEC, SEG), shape(VEC, VEC)),
        compiler_params=params(8),
        name="finish",
    )(gram, projected)
    return basis.T, triangle


def solution(mesh):
    torus = Mesh(mesh.devices.reshape(SIZES), AXES)
    placed = (P(AXES, None), P(AXES, None))
    return jax.shard_map(
        per_device, mesh=torus, in_specs=placed, out_specs=(P(AXES, None), P()), check_vma=False
    )
```

```python
import jax
import jax.numpy as jnp
from jax import lax
from jax.experimental import pallas as pl
from jax.experimental.pallas import tpu as pltpu
from jax.sharding import Mesh
from jax.sharding import PartitionSpec as P

AXES = ("xl", "z", "core", "y", "xh")
SIZES = (2, 8, 2, 4, 2)
ROWS = ("z", "core")
COLS = ("xl", "y", "xh")
CHIPS = 128
HALF = 8
NR = 16
NC = 16
SEG = 256
DIM = 192
VEC = 16
WIDE = DIM + VEC
DEPTH = 6
SCALE = 14.426950408889634
UNSCALE = 4.5399929762484854e-05
EPS = 1e-6
MIB = 1 << 20
F32 = jnp.float32
BF16 = jnp.bfloat16
HI = lax.Precision.HIGHEST


def params(mib):
    return pltpu.CompilerParams(vmem_limit_bytes=mib * MIB)


def vmem():
    return pl.BlockSpec(memory_space=pltpu.VMEM)


def smem():
    return pl.BlockSpec(memory_space=pltpu.SMEM)


def nt(a, b, **kw):
    return lax.dot_general(a, b, (((1,), (1,)), ((), ())), preferred_element_type=F32, **kw)


def unit_kernel(e_ref, v_ref, u_ref, many_ref):
    e = e_ref[...].astype(F32)
    u = (e * lax.rsqrt(jnp.sum(e * e, axis=0, keepdims=True) + EPS)).astype(BF16)
    u_ref[...] = u
    v = v_ref[...].astype(BF16)
    for k in range(NC):
        many_ref[k, 0:DIM, :] = u
        many_ref[k, DIM:WIDE, :] = v


def affinity_kernel(pos_ref, t_ref, *refs):
    pairs, lone = refs[0:7], refs[7:9]
    b_ref, deg_ref, s_ref, sum_ref, done_ref, sem_ref = refs[9:15]
    z, core = pos_ref[0], pos_ref[1]
    step = pl.program_id(0)

    def place(chip, side, rows):
        s_ref[lax.rem(chip + 16, 8) * 2 + side] = rows.T

    @pl.when(step == 0)
    def _():
        sign = 1 - 2 * core
        place(z, core, pairs[0][0])
        place(z, 1 - core, pairs[0][1])
        for k in range(1, 4):
            place(z - k * sign, core, pairs[2 * k - 1][0])
            place(z - k * sign, 1 - core, pairs[2 * k - 1][1])
            place(z + k * sign, 1 - core, pairs[2 * k][0])
            place(z + k * sign, core, pairs[2 * k][1])
        place(z + 4, core, lone[0][...])
        place(z + 4, 1 - core, lone[1][...])

    def store(turn, j):
        slot = lax.rem(turn, 2) * 2 + j
        return pltpu.make_async_copy(done_ref.at[slot], b_ref.at[turn * 2 + j], sem_ref.at[slot])

    for j in range(2):
        pl.when(step >= 2)(lambda: store(step - 2, j).wait())
        slot = lax.rem(step, 2) * 2 + j
        piece = t_ref[step * 2 + j, 0:DIM, :]
        total = jnp.zeros((8, SEG), F32)
        for r in range(NR):
            score = jnp.dot(s_ref[r], piece, preferred_element_type=F32)
            tile = jnp.exp2(score * SCALE)
            total = total + jnp.sum(tile.reshape(SEG // 8, 8, SEG), axis=0)
            done_ref[slot, r * SEG : (r + 1) * SEG, :] = tile.astype(BF16)
        store(step, j).start()
        sums = jnp.sum(total, axis=0, keepdims=True) * UNSCALE
        sum_ref[pl.ds(step * 2 + j, 1), :] = sums

    @pl.when(step == NC // 2 - 1)
    def _():
        for k in range(NC):
            deg_ref[k] = sum_ref[...].astype(BF16)
        for turn in (NC // 2 - 2, NC // 2 - 1):
            for j in range(2):
                store(turn, j).wait()


def apply_kernel(pos_ref, deg_ref, t_ref, b_ref, mine_ref, other_ref, own_ref, root_ref, held_ref, sem_ref):
    def fetch(t):
        slot = t % DEPTH
        return pltpu.make_async_copy(b_ref.at[t], held_ref.at[slot], sem_ref.at[slot])

    for t in range(DEPTH):
        fetch(t).start()
    root_ref[...] = lax.rsqrt(jnp.sum(deg_ref[...].astype(F32), axis=0))
    core = pos_ref[0]
    own_ref[...] = root_ref[pl.ds(pos_ref[1], 1), :] * UNSCALE
    for t in range(NC):
        v = t_ref[t, DIM:WIDE, :].astype(F32)
        w = (v * root_ref[t : t + 1, :]).astype(BF16)
        fetch(t).wait()
        for r in range(NR // 2):
            for side, p_ref in ((core, mine_ref), (1 - core, other_ref)):
                rows = pl.ds(pl.multiple_of((r * 2 + side) * SEG, SEG), SEG)
                part = nt(w, held_ref[t % DEPTH, rows, :])
                p_ref[r] = part if t == 0 else p_ref[r] + part
        if t + DEPTH < NC:
            fetch(t + DEPTH).start()


def project_kernel(p_ref, own_ref, q_ref, gram_ref):
    q = jnp.sum(p_ref[...], axis=0) * own_ref[...]
    q_ref[...] = q
    down = jnp.concatenate([jnp.broadcast_to(q[a : a + 1], (VEC, SEG)) for a in range(VEC)], axis=0)
    pairs = down * jnp.concatenate([q] * VEC, axis=0)
    gram = nt(jnp.ones((8, SEG), F32), pairs, precision=HI)[0:1]
    flat = jnp.concatenate([gram[:, 0:128], gram[:, 128:256]], axis=0)
    gram_ref[...] = flat


def finish_kernel(gram_ref, q_ref, basis_ref, triangle_ref):
    flat = jnp.sum(gram_ref[...], axis=0)
    row = lax.broadcasted_iota(jnp.int32, (VEC, 128), 0)
    lane = lax.broadcasted_iota(jnp.int32, (VEC, 128), 1)
    low = jnp.where(lane // VEC == row, flat[0:1], 0.0)
    high = jnp.where(lane // VEC == row - 8, flat[1:2], 0.0)
    pick = jnp.where(
        lax.broadcasted_iota(jnp.int32, (128, 128), 0) % VEC
        == lax.broadcasted_iota(jnp.int32, (128, 128), 1),
        1.0,
        0.0,
    )
    g = jnp.dot(low + high, pick, preferred_element_type=F32, precision=HI)
    q = q_ref[...]
    wide = lax.broadcasted_iota(jnp.int32, (VEC, SEG), 0)
    for k in range(VEC):
        column = jnp.sum(jnp.where(lane == k, g, 0.0), axis=1, keepdims=True)
        inverse = lax.rsqrt(column[k : k + 1, :])
        factor = column * inverse
        top_g = g[k : k + 1, :] * inverse
        top_q = q[k : k + 1, :] * inverse
        g = jnp.where(row == k, top_g, jnp.where(row > k, g - factor * top_g, g))
        q = jnp.where(wide == k, top_q, jnp.where(wide > k, q - factor * top_q, q))
    basis_ref[...] = q
    triangle_ref[...] = jnp.where(lane >= row, g, 0.0)[:, 0:VEC]


def to_all(copies, axes):
    return lax.all_to_all(copies, axes, split_axis=0, concat_axis=0, tiled=True)


def shape(*dims, dtype=F32):
    return jax.ShapeDtypeStruct(dims, dtype)


def across(a):
    return lax.ppermute(a, "core", [(0, 1), (1, 0)])


def along(a, hops):
    turns = []
    for z in range(8):
        turns += [(z * 2, (z + hops) % 8 * 2), (z * 2 + 1, (z - hops) % 8 * 2 + 1)]
    return lax.ppermute(a, ROWS, turns)


def per_device(embeddings, vectors):
    z, core = lax.axis_index("z"), lax.axis_index("core")
    column = lax.axis_index(COLS)
    unit, unit_copies = pl.pallas_call(
        unit_kernel,
        out_shape=(shape(DIM, SEG, dtype=BF16), shape(NC, WIDE, SEG, dtype=BF16)),
        name="unit",
    )(embeddings.T, vectors.T)
    columns = to_all(unit_copies, COLS)
    pair = jnp.stack([unit, across(unit)])
    one, two = along(pair, 1), along(pair, 2)
    three, four = along(two, 1), along(two[0], 2)
    pairs = (pair, one, across(one), two, across(two), three, across(three))
    block, degree = pl.pallas_call(
        affinity_kernel,
        grid=(NC // 2,),
        out_shape=(pltpu.HBM((NC, NR * SEG, SEG), BF16), shape(NC, NC, SEG, dtype=BF16)),
        in_specs=[smem()] + [vmem()] * 10,
        out_specs=(pl.BlockSpec(memory_space=pl.ANY), vmem()),
        scratch_shapes=[
            pltpu.VMEM((NR, SEG, DIM), BF16),
            pltpu.VMEM((NC, SEG), F32),
            pltpu.VMEM((4, NR * SEG, SEG), BF16),
            pltpu.SemaphoreType.DMA((4,)),
        ],
        compiler_params=params(32),
        cost_estimate=pl.CostEstimate(
            flops=2 * 256 * 4096 * 4096, transcendentals=4096 * 4096, bytes_accessed=1 << 25
        ),
        name="affinity",
    )(jnp.stack([z, core]), columns, *pairs, four, across(four))
    degree = to_all(degree, COLS)
    mine, other, own = pl.pallas_call(
        apply_kernel,
        out_shape=(shape(HALF, VEC, SEG), shape(HALF, VEC, SEG), shape(1, SEG)),
        in_specs=[smem(), vmem(), vmem(), pl.BlockSpec(memory_space=pl.ANY)],
        out_specs=(vmem(), vmem(), vmem()),
        scratch_shapes=[
            pltpu.VMEM((NC, SEG), F32),
            pltpu.VMEM((DEPTH, NR * SEG, SEG), BF16),
            pltpu.SemaphoreType.DMA((DEPTH,)),
        ],
        compiler_params=params(44),
        name="apply",
    )(jnp.stack([core, column]), degree, columns, block)
    product = to_all(mine + across(other), "z")
    projected, gram = pl.pallas_call(
        project_kernel,
        out_shape=(shape(VEC, SEG), shape(2, 128)),
        compiler_params=params(8),
        name="project",
    )(product, own)
    gram = jnp.broadcast_to(gram + across(gram), (CHIPS, 2, 128))
    gram = to_all(gram, ("xl", "z", "y", "xh"))
    basis, triangle = pl.pallas_call(
        finish_kernel,
        out_shape=(shape(VEC, SEG), shape(VEC, VEC)),
        compiler_params=params(8),
        name="finish",
    )(gram, projected)
    return basis.T, triangle


def solution(mesh):
    torus = Mesh(mesh.devices.reshape(SIZES), AXES)
    placed = (P(AXES, None), P(AXES, None))
    return jax.shard_map(
        per_device, mesh=torus, in_specs=placed, out_specs=(P(AXES, None), P()), check_vma=False
    )
```

```python
import jax
import jax.numpy as jnp
from jax import lax
from jax.experimental import pallas as pl
from jax.experimental.pallas import tpu as pltpu
from jax.sharding import Mesh
from jax.sharding import PartitionSpec as P

AXES = ("xl", "z", "core", "y", "xh")
SIZES = (2, 8, 2, 4, 2)
ROWS = ("z", "core")
COLS = ("xl", "y", "xh")
CHIPS = 128
HALF = 8
NR = 16
NC = 16
SEG = 256
DIM = 192
VEC = 16
WIDE = DIM + VEC
DEPTH = 4
SCALE = 14.426950408889634
UNSCALE = 4.5399929762484854e-05
EPS = 1e-6
MIB = 1 << 20
F32 = jnp.float32
BF16 = jnp.bfloat16
HI = lax.Precision.HIGHEST


def params(mib):
    return pltpu.CompilerParams(vmem_limit_bytes=mib * MIB)


def vmem():
    return pl.BlockSpec(memory_space=pltpu.VMEM)


def smem():
    return pl.BlockSpec(memory_space=pltpu.SMEM)


def nt(a, b, **kw):
    return lax.dot_general(a, b, (((1,), (1,)), ((), ())), preferred_element_type=F32, **kw)


def unit_kernel(e_ref, v_ref, u_ref, many_ref):
    e = e_ref[...].astype(F32)
    u = (e * lax.rsqrt(jnp.sum(e * e, axis=0, keepdims=True) + EPS)).astype(BF16)
    u_ref[...] = u
    v = v_ref[...].astype(BF16)
    for k in range(NC):
        many_ref[k, 0:DIM, :] = u
        many_ref[k, DIM:WIDE, :] = v


def affinity_kernel(pos_ref, t_ref, *refs):
    pairs, lone = refs[0:7], refs[7:9]
    b_ref, deg_ref, s_ref, sum_ref, done_ref, sem_ref = refs[9:15]
    z, core = pos_ref[0], pos_ref[1]
    step = pl.program_id(0)

    def place(chip, side, rows):
        s_ref[lax.rem(chip + 16, 8) * 2 + side] = rows.T

    @pl.when(step == 0)
    def _():
        sign = 1 - 2 * core
        place(z, core, pairs[0][0])
        place(z, 1 - core, pairs[0][1])
        for k in range(1, 4):
            place(z - k * sign, core, pairs[2 * k - 1][0])
            place(z - k * sign, 1 - core, pairs[2 * k - 1][1])
            place(z + k * sign, 1 - core, pairs[2 * k][0])
            place(z + k * sign, core, pairs[2 * k][1])
        place(z + 4, core, lone[0][...])
        place(z + 4, 1 - core, lone[1][...])

    def store(turn, j):
        slot = lax.rem(turn, 2) * 2 + j
        return pltpu.make_async_copy(done_ref.at[slot], b_ref.at[turn * 2 + j], sem_ref.at[slot])

    for j in range(2):
        pl.when(step >= 2)(lambda: store(step - 2, j).wait())
        slot = lax.rem(step, 2) * 2 + j
        piece = t_ref[step * 2 + j, 0:DIM, :]
        total = jnp.zeros((8, SEG), F32)
        for r in range(NR):
            score = jnp.dot(s_ref[r], piece, preferred_element_type=F32)
            tile = jnp.exp2(score * SCALE)
            total = total + jnp.sum(tile.reshape(SEG // 8, 8, SEG), axis=0)
            done_ref[slot, r * SEG : (r + 1) * SEG, :] = tile.astype(BF16)
        store(step, j).start()
        sums = jnp.sum(total, axis=0, keepdims=True) * UNSCALE
        sum_ref[pl.ds(step * 2 + j, 1), :] = sums

    @pl.when(step == NC // 2 - 1)
    def _():
        for k in range(NC):
            deg_ref[k] = sum_ref[...].astype(BF16)
        for turn in (NC // 2 - 2, NC // 2 - 1):
            for j in range(2):
                store(turn, j).wait()


def apply_kernel(pos_ref, deg_ref, t_ref, b_ref, mine_ref, other_ref, own_ref, root_ref, held_ref, sem_ref):
    def fetch(t):
        slot = t % DEPTH
        return pltpu.make_async_copy(b_ref.at[t], held_ref.at[slot], sem_ref.at[slot])

    for t in range(DEPTH):
        fetch(t).start()
    root_ref[...] = lax.rsqrt(jnp.sum(deg_ref[...].astype(F32), axis=0))
    core = pos_ref[0]
    own_ref[...] = root_ref[pl.ds(pos_ref[1], 1), :] * UNSCALE
    for t in range(NC):
        v = t_ref[t, DIM:WIDE, :].astype(F32)
        w = (v * root_ref[t : t + 1, :]).astype(BF16)
        fetch(t).wait()
        for r in range(NR // 2):
            for side, p_ref in ((core, mine_ref), (1 - core, other_ref)):
                rows = pl.ds(pl.multiple_of((r * 2 + side) * SEG, SEG), SEG)
                part = nt(w, held_ref[t % DEPTH, rows, :])
                p_ref[r] = part if t == 0 else p_ref[r] + part
        if t + DEPTH < NC:
            fetch(t + DEPTH).start()


def project_kernel(p_ref, own_ref, q_ref, gram_ref):
    q = jnp.sum(p_ref[...], axis=0) * own_ref[...]
    q_ref[...] = q
    down = jnp.concatenate([jnp.broadcast_to(q[a : a + 1], (VEC, SEG)) for a in range(VEC)], axis=0)
    pairs = down * jnp.concatenate([q] * VEC, axis=0)
    gram = nt(jnp.ones((8, SEG), F32), pairs, precision=HI)[0:1]
    flat = jnp.concatenate([gram[:, 0:128], gram[:, 128:256]], axis=0)
    gram_ref[...] = flat


def finish_kernel(gram_ref, q_ref, basis_ref, triangle_ref):
    flat = jnp.sum(gram_ref[...], axis=0)
    row = lax.broadcasted_iota(jnp.int32, (VEC, 128), 0)
    lane = lax.broadcasted_iota(jnp.int32, (VEC, 128), 1)
    low = jnp.where(lane // VEC == row, flat[0:1], 0.0)
    high = jnp.where(lane // VEC == row - 8, flat[1:2], 0.0)
    pick = jnp.where(
        lax.broadcasted_iota(jnp.int32, (128, 128), 0) % VEC
        == lax.broadcasted_iota(jnp.int32, (128, 128), 1),
        1.0,
        0.0,
    )
    g = jnp.dot(low + high, pick, preferred_element_type=F32, precision=HI)
    q = q_ref[...]
    wide = lax.broadcasted_iota(jnp.int32, (VEC, SEG), 0)
    for k in range(VEC):
        column = jnp.sum(jnp.where(lane == k, g, 0.0), axis=1, keepdims=True)
        inverse = lax.rsqrt(column[k : k + 1, :])
        factor = column * inverse
        top_g = g[k : k + 1, :] * inverse
        top_q = q[k : k + 1, :] * inverse
        g = jnp.where(row == k, top_g, jnp.where(row > k, g - factor * top_g, g))
        q = jnp.where(wide == k, top_q, jnp.where(wide > k, q - factor * top_q, q))
    basis_ref[...] = q
    triangle_ref[...] = jnp.where(lane >= row, g, 0.0)[:, 0:VEC]


def to_all(copies, axes):
    return lax.all_to_all(copies, axes, split_axis=0, concat_axis=0, tiled=True)


def shape(*dims, dtype=F32):
    return jax.ShapeDtypeStruct(dims, dtype)


def across(a):
    return lax.ppermute(a, "core", [(0, 1), (1, 0)])


def along(a, hops):
    turns = []
    for z in range(8):
        turns += [(z * 2, (z + hops) % 8 * 2), (z * 2 + 1, (z - hops) % 8 * 2 + 1)]
    return lax.ppermute(a, ROWS, turns)


def per_device(embeddings, vectors):
    z, core = lax.axis_index("z"), lax.axis_index("core")
    column = lax.axis_index(COLS)
    unit, unit_copies = pl.pallas_call(
        unit_kernel,
        out_shape=(shape(DIM, SEG, dtype=BF16), shape(NC, WIDE, SEG, dtype=BF16)),
        name="unit",
    )(embeddings.T, vectors.T)
    columns = to_all(unit_copies, COLS)
    pair = jnp.stack([unit, across(unit)])
    one, two = along(pair, 1), along(pair, 2)
    three, four = along(two, 1), along(two[0], 2)
    pairs = (pair, one, across(one), two, across(two), three, across(three))
    block, degree = pl.pallas_call(
        affinity_kernel,
        grid=(NC // 2,),
        out_shape=(pltpu.HBM((NC, NR * SEG, SEG), BF16), shape(NC, NC, SEG, dtype=BF16)),
        in_specs=[smem()] + [vmem()] * 10,
        out_specs=(pl.BlockSpec(memory_space=pl.ANY), vmem()),
        scratch_shapes=[
            pltpu.VMEM((NR, SEG, DIM), BF16),
            pltpu.VMEM((NC, SEG), F32),
            pltpu.VMEM((4, NR * SEG, SEG), BF16),
            pltpu.SemaphoreType.DMA((4,)),
        ],
        compiler_params=params(32),
        cost_estimate=pl.CostEstimate(
            flops=2 * 256 * 4096 * 4096, transcendentals=4096 * 4096, bytes_accessed=1 << 25
        ),
        name="affinity",
    )(jnp.stack([z, core]), columns, *pairs, four, across(four))
    degree = to_all(degree, COLS)
    mine, other, own = pl.pallas_call(
        apply_kernel,
        out_shape=(shape(HALF, VEC, SEG), shape(HALF, VEC, SEG), shape(1, SEG)),
        in_specs=[smem(), vmem(), vmem(), pl.BlockSpec(memory_space=pl.ANY)],
        out_specs=(vmem(), vmem(), vmem()),
        scratch_shapes=[
            pltpu.VMEM((NC, SEG), F32),
            pltpu.VMEM((DEPTH, NR * SEG, SEG), BF16),
            pltpu.SemaphoreType.DMA((DEPTH,)),
        ],
        compiler_params=params(44),
        name="apply",
    )(jnp.stack([core, column]), degree, columns, block)
    product = to_all(mine + across(other), "z")
    projected, gram = pl.pallas_call(
        project_kernel,
        out_shape=(shape(VEC, SEG), shape(2, 128)),
        compiler_params=params(8),
        name="project",
    )(product, own)
    gram = jnp.broadcast_to(gram + across(gram), (CHIPS, 2, 128))
    gram = to_all(gram, ("xl", "z", "y", "xh"))
    basis, triangle = pl.pallas_call(
        finish_kernel,
        out_shape=(shape(VEC, SEG), shape(VEC, VEC)),
        compiler_params=params(8),
        name="finish",
    )(gram, projected)
    return basis.T, triangle


def solution(mesh):
    torus = Mesh(mesh.devices.reshape(SIZES), AXES)
    placed = (P(AXES, None), P(AXES, None))
    return jax.shard_map(
        per_device, mesh=torus, in_specs=placed, out_specs=(P(AXES, None), P()), check_vma=False
    )
```
